32 devices in a mesh: pb: 2 (over x), row: 16 (over z, y, core).
Axes of the slice: x: 2, y: 2, z: 4, core: 2. Of those that a mesh axis runs over, the one named last changes fastest.
Arguments:
- force_constants: float32 [9, 4608, 4608], P(None, 'row', 'pb'), may hold values from -0.1 to 3.6, as said below
- offsets: int32 [9, 3], replicated, may hold values from -2 to 2, as said below
- qpoints: int32 [2, 3], replicated, may hold values from 0 to 7
- lower_bound: float32 [2], P('pb'), may hold values from 1.5 to 2.5
- upper_bound: float32 [2], P('pb'), may hold values from 5.5 to 6.5
- start_vectors: float32 [4608, 128], P('row'), may hold values from -6 to 6
Outputs:
- basis: float32 [2, 4608, 128], P('pb', 'row')
- ritz: float32 [2, 64, 128], P('pb')
The draws below stay inside these ranges and needn't reach their ends.
Inputs may be any that keep to these rules, and one draw needn't show every extreme that they name: `force_constants`: cell 0 is symmetric; for 1 <= c <= 4, cell c + 4 is the transpose of cell c, so every D(q) is Hermitian. `offsets`: row 0 is zero; for 1 <= c <= 4, row c + 4 is the negative of row c.
All inputs are finite; a program needn't handle non-finite values.
Results may differ from the reference program's by a relative error of at most 0.00025.
Values sent between devices are 32-bit elements; how exact they have to be, the bound alone decides.
A program may use at most 128 MiB of HBM per device.

```python
import math
import jax
import jax.numpy as jnp
from jax import lax

MODES = 4608
VECTORS = 64
PAIRS = 4
DEG = 2
QDEN = 8
QPTS = 2


def draw_force_constants(key, part):
    sigma = 0.2 / math.sqrt(MODES)
    noise_key = jax.random.fold_in(key, 11)
    diag_key = jax.random.fold_in(key, 13)
    base = jnp.clip(jax.random.normal(noise_key, (PAIRS + 1, MODES, MODES), jnp.float32), -6.0, 6.0) * sigma
    diagonal = jax.random.uniform(diag_key, (MODES,), jnp.float32, 1.5, 3.5)
    home_cell = 0.5 * (base[0] + base[0].T) + jnp.diag(diagonal)
    return jnp.concatenate([home_cell[None], base[1:], jnp.transpose(base[1:], (0, 2, 1))], axis=0)


def draw_offsets(key, part):
    paired = jax.random.randint(jax.random.fold_in(key, 17), (PAIRS, 3), -2, 3, jnp.int32)
    return jnp.concatenate([jnp.zeros((1, 3), jnp.int32), paired, -paired], axis=0)


def with_ends(values, key, smallest, largest):
    shape = values.shape
    index_at = [jax.random.randint(jax.random.fold_in(key, axis), (), 0, shape[axis]) for axis in range(len(shape))]
    values = values.at[tuple(index_at)].set(smallest)
    longest = shape.index(max(shape))
    index_at[longest] = (index_at[longest] + 1) % shape[longest]
    return values.at[tuple(index_at)].set(largest)


def shard_levels(stream_key, dims, shards, low, largest):
    level, own = 1.0, jax.random.fold_in(stream_key, 6)
    for axis_at, blocks in shards:
        heights = jnp.exp(jax.random.uniform(jax.random.fold_in(own, axis_at), (blocks,), jnp.float32, low / len(shards), largest / len(shards)))
        level = level * jnp.repeat(heights, dims[axis_at] // blocks).reshape([-1 if axis == axis_at else 1 for axis in range(len(dims))])
    return level


def normal_values(key, shape, deviation, reach, split=(), kind=jnp.bfloat16):
    values = jax.random.normal(key, shape, jnp.float32) * deviation
    if len(split) > 0:
        values = shard_levels(key, shape, split, -0.22, 0.18) * values
    return jnp.clip(values, min=-reach, max=reach).astype(kind)


def setup_inputs(seed: int = 0) -> dict:
    splits = jax.random.split(jax.random.key(seed), 7)
    force_constants = draw_force_constants(jax.random.fold_in(splits[6], 71), 0)
    offsets = draw_offsets(jax.random.fold_in(splits[6], 71), 0)
    qpoints = with_ends(jax.random.randint(splits[2], (QPTS, 3), 0, QDEN), jax.random.fold_in(splits[2], 1), 0, QDEN - 1).astype(jnp.int32)
    lower_bound = jnp.clip(1.5 + 1.0 * jax.random.uniform(splits[3], (QPTS,), jnp.float32) ** shard_levels(splits[3], (QPTS,), ((0, 2),), -0.2, 0.2), 1.5, 2.5)
    upper_bound = jnp.clip(5.5 + 1.0 * jax.random.uniform(splits[4], (QPTS,), jnp.float32) ** shard_levels(splits[4], (QPTS,), ((0, 2),), -0.2, 0.2), 5.5, 6.5)
    start_vectors = normal_values(splits[5], (MODES, 2 * VECTORS), 1.0, 6.0, ((0, 16),), jnp.float32)
    return dict(force_constants=force_constants, offsets=offsets, qpoints=qpoints, lower_bound=lower_bound, upper_bound=upper_bound, start_vectors=start_vectors)


highest = lax.Precision.HIGHEST

def product(left, right):
    return jnp.dot(left.astype(jnp.float32), right.astype(jnp.float32), precision=highest, preferred_element_type=jnp.float32)

def inner_product(left, right):
    return lax.dot_general(left.astype(jnp.float32), right.astype(jnp.float32), (((0,), (0,)), ((), ())), precision=highest, preferred_element_type=jnp.float32)

def complex_times(left_real, left_imag, right_real, right_imag):
    return (product(left_real, right_real) - product(left_imag, right_imag), product(left_real, right_imag) + product(left_imag, right_real))

def phase_table(qpoints, offsets):
    turns = lax.optimization_barrier(jnp.sum(qpoints[:, None, :] * offsets[None, :, :], axis=2))
    turns = jnp.mod(turns, QDEN)
    angle = 2.0 * math.pi / QDEN * turns.astype(jnp.float32)
    return jnp.stack([jnp.cos(angle), jnp.sin(angle)], axis=1)

def factor_inverse(gram_real, gram_imag):
    order_size = gram_real.shape[0]
    embedded = jnp.stack([jnp.stack([gram_real, -gram_imag], axis=2), jnp.stack([gram_imag, gram_real], axis=2)], axis=1).reshape(2 * order_size, 2 * order_size)
    lower_factor = jnp.linalg.cholesky(embedded)
    identity = jnp.eye(2 * order_size, dtype=gram_real.dtype)
    inverse = jax.scipy.linalg.solve_triangular(lower_factor, identity, lower=True)
    blocks = inverse.reshape(order_size, 2, order_size, 2)
    return (blocks[:, 0, :, 0], blocks[:, 1, :, 0])

def right_block(inverse_real, inverse_imag):
    upper_half = jnp.concatenate([inverse_real.T, -inverse_imag.T], axis=1)
    lower_half = jnp.concatenate([inverse_imag.T, inverse_real.T], axis=1)
    return jnp.concatenate([upper_half, lower_half], axis=0)

def split_gram(matrix, vector_count):
    return (matrix[:vector_count, :vector_count] + matrix[vector_count:, vector_count:], matrix[:vector_count, vector_count:] - matrix[vector_count:, :vector_count])

def chebyshev(vectors, apply_matrix, lower_value, upper_value):
    centre = 0.5 * (upper_value + lower_value)
    spread = 0.5 * (upper_value - lower_value)
    previous = vectors
    current = (apply_matrix(vectors) - centre * vectors) / spread
    for repeat in range(DEG - 1):
        following = 2.0 * (apply_matrix(current) - centre * current) / spread - previous
        previous, current = (current, following)
    return current

def reference(force_constants, offsets, qpoints, lower_bound, upper_bound, start_vectors):
    cell_count = force_constants.shape[0]
    vector_count = start_vectors.shape[1] // 2
    coefficients = phase_table(qpoints, offsets)
    flat_constants = force_constants.reshape(cell_count, MODES * MODES)

    def one_point(point):
        dynamic = product(coefficients[point], flat_constants).reshape(2, MODES, MODES)
        dyn_real = dynamic[0]
        dyn_imag = dynamic[1]

        def apply_matrix(vectors):
            part_real = product(dyn_real, vectors)
            part_imag = product(dyn_imag, vectors)
            return jnp.concatenate([part_real[:, :vector_count] - part_imag[:, vector_count:], part_real[:, vector_count:] + part_imag[:, :vector_count]], axis=1)
        lower_value = lower_bound[point]
        upper_value = upper_bound[point]
        first_pass = chebyshev(start_vectors, apply_matrix, lower_value, upper_value)
        final_pass = chebyshev(first_pass, apply_matrix, lower_value, upper_value)
        image = apply_matrix(final_pass)
        over_real, over_imag = split_gram(inner_product(final_pass, final_pass), vector_count)
        proj_real, proj_imag = split_gram(inner_product(final_pass, image), vector_count)
        inverse_real, inverse_imag = factor_inverse(over_real, over_imag)
        basis_point = math.sqrt(MODES) * product(final_pass, right_block(inverse_real, inverse_imag))
        temp_real, temp_imag = complex_times(proj_real, proj_imag, inverse_real.T, -inverse_imag.T)
        ritz_real, ritz_imag = complex_times(inverse_real, inverse_imag, temp_real, temp_imag)
        return (basis_point, jnp.concatenate([ritz_real, ritz_imag], axis=1))
    basis, ritz = lax.map(one_point, jnp.arange(QPTS, dtype=jnp.int32))
    return (basis, ritz)
```

```python
import functools
import math

import jax
import jax.numpy as jnp
from jax import lax
from jax.experimental import pallas as pl
from jax.experimental.pallas import tpu as pltpu
from jax.sharding import PartitionSpec as P

MODES = 4608
QDEN = 8


highest = lax.Precision.HIGHEST


def product(left, right):
    return jnp.dot(left, right, precision=highest, preferred_element_type=jnp.float32)


def inner_product(left, right):
    return lax.dot_general(
        left, right, (((0,), (0,)), ((), ())), precision=highest, preferred_element_type=jnp.float32
    )


def complex_times(left_real, left_imag, right_real, right_imag):
    return (
        product(left_real, right_real) - product(left_imag, right_imag),
        product(left_real, right_imag) + product(left_imag, right_real),
    )


def phase_table(qpoints, offsets):
    turns = jnp.sum(qpoints[:, None, :] * offsets[None, :, :], axis=2)
    turns = jnp.mod(turns, QDEN)
    angle = 2.0 * math.pi / QDEN * turns.astype(jnp.float32)
    return jnp.stack([jnp.cos(angle), jnp.sin(angle)], axis=1)


def factor_inverse(gram_real, gram_imag):
    order_size = gram_real.shape[0]
    embedded = jnp.stack(
        [jnp.stack([gram_real, -gram_imag], axis=2), jnp.stack([gram_imag, gram_real], axis=2)],
        axis=1,
    ).reshape(2 * order_size, 2 * order_size)
    lower_factor = jnp.linalg.cholesky(embedded)
    identity = jnp.eye(2 * order_size, dtype=gram_real.dtype)
    inverse = jax.scipy.linalg.solve_triangular(lower_factor, identity, lower=True)
    blocks = inverse.reshape(order_size, 2, order_size, 2)
    return (blocks[:, 0, :, 0], blocks[:, 1, :, 0])


def right_block(inverse_real, inverse_imag):
    upper_half = jnp.concatenate([inverse_real.T, -inverse_imag.T], axis=1)
    lower_half = jnp.concatenate([inverse_imag.T, inverse_real.T], axis=1)
    return jnp.concatenate([upper_half, lower_half], axis=0)


def split_gram(matrix, vector_count):
    return (
        matrix[:vector_count, :vector_count] + matrix[vector_count:, vector_count:],
        matrix[:vector_count, vector_count:] - matrix[vector_count:, :vector_count],
    )


def combine_parts(part_real, part_imag, vector_count):
    return jnp.concatenate(
        [
            part_real[:, :vector_count] - part_imag[:, vector_count:],
            part_real[:, vector_count:] + part_imag[:, :vector_count],
        ],
        axis=1,
    )


def chebyshev(vectors, apply_matrix, lower_value, upper_value, first_image):
    centre = 0.5 * (upper_value + lower_value)
    spread = 0.5 * (upper_value - lower_value)
    previous = vectors
    first_image = apply_matrix(vectors)
    current = (first_image - centre * vectors) / spread
    following = 2.0 * (apply_matrix(current) - centre * current) / spread - previous
    previous, current = (current, following)
    return current


def on_device(force_constants, offsets, qpoints, lower_bound, upper_bound, start_vectors):
    cell_count, row_count, col_count = force_constants.shape
    qcount = qpoints.shape[0]
    vector_count = start_vectors.shape[1] // 2
    coefficients = phase_table(qpoints, offsets).reshape(2 * qcount, cell_count)
    partial_value = product(
        coefficients, force_constants.reshape(cell_count, row_count * col_count)
    )
    partial_value = partial_value.reshape(qcount, 2, row_count, col_count)
    owned_block = lax.all_to_all(partial_value, "pb", split_axis=0, concat_axis=3, tiled=True)
    dyn_real = owned_block[0, 0]
    dyn_imag = owned_block[0, 1]

    def accumulate(piece):
        return combine_parts(product(dyn_real, piece), product(dyn_imag, piece), vector_count)

    def apply_matrix(vectors):
        return accumulate(lax.all_gather(vectors, "row", axis=0, tiled=True))

    lower_value = lower_bound[0]
    upper_value = upper_bound[0]
    first_pass = chebyshev(start_vectors, apply_matrix, lower_value, upper_value, None)
    final_pass = chebyshev(first_pass, apply_matrix, lower_value, upper_value, None)
    image = apply_matrix(final_pass)
    over_total, proj_total = lax.psum(
        (inner_product(final_pass, final_pass), inner_product(final_pass, image)), "row"
    )
    over_real, over_imag = split_gram(over_total, vector_count)
    proj_real, proj_imag = split_gram(proj_total, vector_count)
    inverse_real, inverse_imag = factor_inverse(over_real, over_imag)
    basis_local = math.sqrt(MODES) * product(final_pass, right_block(inverse_real, inverse_imag))
    temp_real, temp_imag = complex_times(proj_real, proj_imag, inverse_real.T, -inverse_imag.T)
    ritz_real, ritz_imag = complex_times(inverse_real, inverse_imag, temp_real, temp_imag)
    ritz_local = jnp.concatenate([ritz_real, ritz_imag], axis=1)
    return (basis_local[None], ritz_local[None])


STEPS = 5
PIECES = 2
TILE = 48
FAR, NEAR, ACROSS_Y, ACROSS_C, RELAY_C = 0, 2, 3, 5, 7
KINDS = 9
MESH = pl.DeviceIdType.MESH


def sign_row(first, second):
    lane = lax.broadcasted_iota(jnp.int32, (1, 128), 1)
    return jnp.where(lane < 64, first, second).astype(jnp.float32)


def eighth_cosine(turn):
    turn = turn & (QDEN - 1)
    half = math.sqrt(0.5)
    value = jnp.float32(0.0)
    for index, exact in enumerate((1.0, half, 0.0, -half, -1.0, -half, 0.0, half)):
        value = jnp.where(turn == index, jnp.float32(exact), value)
    return value


def filter_kernel(
    offsets_ref, qpoints_ref, lower_ref, upper_ref, force_ref, start_ref, final_ref, gram_ref,
    tiles, high, low, full, own, part, other, split, bounds, partner_bounds, sums, arrived,
    tile_sem, send_sem, recv_sem, x_send, x_recv, b_sem, g_send, g_recv,
):
    p = lax.axis_index("pb")
    row = lax.axis_index("row")
    rows = start_ref.shape[0]
    cells = force_ref.shape[0]
    cols = force_ref.shape[2]
    pairs = (cells - 1) // 2
    points = 2
    depth = rows // PIECES
    z, y, c = row // 4, (row // 2) % 2, row % 2
    group = z // 2
    owner = group == p
    not_owner = group != p
    level = z % 2
    far_piece = group + p - 2 * group * p
    to_x = (1 - p, row)
    to_c = (p, row + 1 - 2 * c)
    to_y = (p, row + 2 - 4 * y)
    to_a = (p, row + 4 - 8 * level)
    to_b = (p, (3 - z) * 4 + y * 2 + c)
    opposite = 2 - 2 * group
    to_far = [(group, (opposite + n) * 4 + y * 2 + c) for n in (0, 1)]
    mine = level * 4 + y * 2 + c

    def tile_copy(index, slot):
        where = pl.ds(pl.multiple_of(index * TILE, 8), TILE)
        return pltpu.make_async_copy(
            force_ref.at[:, where, :], tiles.at[slot], tile_sem.at[slot]
        )

    tile_copy(0, 0).start()
    tile_copy(1, 1).start()

    own[0, 0] = start_ref[...]
    own[0, 1] = start_ref[...]
    own[1] = jnp.zeros((points, rows, 128), jnp.float32)
    centre = 0.5 * (upper_ref[0] + lower_ref[0])
    spread = 0.5 * (upper_ref[0] - lower_ref[0])
    line = lax.broadcasted_iota(jnp.int32, (8, 128), 0)
    bounds[...] = jnp.where(line < 4, centre, spread)

    def block_rows(index, piece=0, count=rows):
        return pl.ds(pl.multiple_of(index * rows + piece * depth, 8), count)

    @pl.when(owner)
    def _():
        full[0, 0, block_rows(mine), :] = start_ref[...]

    barrier = pltpu.get_barrier_semaphore()
    around = [to_x, to_c, to_y, to_a]
    around += [(q, (opposite + n) * 4 + y * 2 + c) for q in (0, 1) for n in (0, 1)]
    for target in around:
        pl.semaphore_signal(barrier, inc=1, device_id=target, device_id_type=MESH)
    pl.semaphore_wait(barrier, len(around))

    bound_copy = pltpu.make_async_remote_copy(
        src_ref=bounds, dst_ref=partner_bounds, send_sem=b_sem.at[0], recv_sem=b_sem.at[1],
        device_id=to_x, device_id_type=MESH,
    )

    def send(slot, q, index, piece, kind, target, at=None):
        view = full.at[slot, q, block_rows(index, piece, depth)]
        source = view
        if kind <= NEAR:
            source = own.at[slot, q, pl.ds(pl.multiple_of(piece * depth, 8), depth)]
        return pltpu.make_async_remote_copy(
            src_ref=source, dst_ref=view,
            send_sem=send_sem.at[q, kind, piece if at is None else at],
            recv_sem=recv_sem.at[slot, q, index, piece],
            device_id=target, device_id_type=MESH,
        )

    def index_of(flipped_level, flipped_y, flipped_c):
        zz = 1 - level if flipped_level else level
        yy = 1 - y if flipped_y else y
        cc = 1 - c if flipped_c else c
        return zz * 4 + yy * 2 + cc

    def far_sends(slot, q):
        return [send(slot, q, mine, far_piece, FAR + n, to_far[n], 0) for n in (0, 1)]

    def near_send(slot, q, piece):
        return send(slot, q, mine, piece, NEAR, to_a)

    def lane_sends(slot, q, which, piece):
        index = index_of(which == 1, False, False)
        return (
            send(slot, q, index, piece, ACROSS_Y + which, to_y),
            send(slot, q, index, piece, ACROSS_C + which, to_c),
        )

    def relay_send(slot, q, which, piece):
        return send(slot, q, index_of(which == 1, True, False), piece, RELAY_C + which, to_c)

    def await_block(slot, q, index, piece):
        send(slot, q, index, piece, ACROSS_C, to_c).wait_recv()

    def direct(slot, q, piece):
        @pl.when(far_piece == piece)
        def _():
            for copy in far_sends(slot, q):
                copy.start()

        @pl.when(owner)
        def _():
            near_send(slot, q, piece).start()
            for copy in lane_sends(slot, q, 0, piece):
                copy.start()

    def lanes(slot, q):
        for piece in range(PIECES):
            @pl.when(not_owner)
            def _():
                await_block(slot, q, index_of(False, False, False), piece)
                for copy in lane_sends(slot, q, 0, piece):
                    copy.start()

            await_block(slot, q, index_of(True, False, False), piece)
            for copy in lane_sends(slot, q, 1, piece):
                copy.start()

    def relays(slot, q):
        for piece in range(PIECES):
            for which in (0, 1):
                await_block(slot, q, index_of(which == 1, True, False), piece)
                relay_send(slot, q, which, piece).start()

    def collect(slot, q):
        for flipped_y in (False, True):
            for piece in range(PIECES):
                for which in (False, True):
                    await_block(slot, q, index_of(which, flipped_y, True), piece)

    def await_sends(slot, q):
        for copy in far_sends(slot, q):
            copy.wait_send()
        for piece in range(PIECES):
            pl.when(owner)(near_send(slot, q, piece).wait_send)
            for which in (0, 1):
                for copy in lane_sends(slot, q, which, piece):
                    copy.wait_send()
                relay_send(slot, q, which, piece).wait_send()

    def partial_copy(slot, q, piece):
        where = pl.ds(piece * depth, depth)
        return pltpu.make_async_remote_copy(
            src_ref=part.at[q, where], dst_ref=other.at[slot, q, where],
            send_sem=x_send.at[q, piece], recv_sem=x_recv.at[slot, q, piece],
            device_id=to_x, device_id_type=MESH,
        )

    def divide(slot, q):
        values = full[slot, q]
        upper = values.astype(jnp.bfloat16)
        split[:, :128] = upper
        split[:, 128:] = (values - upper.astype(jnp.float32)).astype(jnp.bfloat16)

    def multiply(q, piece):
        def stacked(ref):
            return ref[q, piece].reshape(2 * depth, cols)

        wide = jnp.dot(stacked(high), split[...], preferred_element_type=jnp.float32)
        rest = jnp.dot(stacked(low), split[:, :128], preferred_element_type=jnp.float32)
        image = wide[:, :128] + (wide[:, 128:] + rest)
        part[q, piece * depth:(piece + 1) * depth] = (
            image[:depth] + sign_row(-1.0, 1.0) * pltpu.roll(image[depth:], 64, 1)
        )

    def update(slot, q, piece, weight, keep):
        mine_q = p == q
        where = slice(piece * depth, (piece + 1) * depth)
        centre = jnp.where(mine_q, bounds[0:1, :], partner_bounds[0:1, :])
        spread = jnp.where(mine_q, bounds[4:5, :], partner_bounds[4:5, :])
        current = own[slot, q, where]
        previous = own[1 - slot, q, where]
        image = part[q, where] + other[slot, q, where]
        following = (image - centre * current) * (weight / spread) - jnp.where(keep, previous, 0.0)
        own[1 - slot, q, where] = following

        @pl.when(owner)
        def _():
            full[1 - slot, q, block_rows(mine, piece, depth), :] = following

    turns = [
        [
            sum(qpoints_ref[q, n] * offsets_ref[n, 1 + pair] for n in range(3))
            for pair in range(pairs)
        ]
        for q in range(points)
    ]
    cosines = [[eighth_cosine(turn) for turn in turns[q]] for q in range(points)]
    sines = [[eighth_cosine(turn - QDEN // 4) for turn in turns[q]] for q in range(points)]

    def assemble(tile, carry):
        slot = tile % 2
        tile_copy(tile, slot).wait()
        piece = tile * TILE // depth
        place = pl.ds(pl.multiple_of(tile * TILE - piece * depth, 16), TILE)
        width = 256
        for at in range(cols // width):
            span = slice(at * width, (at + 1) * width)
            real = [tiles[slot, 0, :, span]] * points
            imag = [None] * points
            for pair in range(pairs):
                first = tiles[slot, 1 + pair, :, span]
                second = tiles[slot, 1 + pair + pairs, :, span]
                total, difference = first + second, first - second
                for q in range(points):
                    real[q] = real[q] + cosines[q][pair] * total
                    term = sines[q][pair] * difference
                    imag[q] = term if pair == 0 else imag[q] + term
            for q in range(points):
                for which, value in ((0, real[q]), (1, imag[q])):
                    upper = value.astype(jnp.bfloat16)
                    high[q, piece, which, place, span] = upper
                    rest = (value - upper.astype(jnp.float32)).astype(jnp.bfloat16)
                    low[q, piece, which, place, span] = rest

        @pl.when(tile + 2 < rows // TILE)
        def _():
            tile_copy(tile + 2, slot).start()

        return carry

    bound_copy.start()
    for piece in range(PIECES):
        direct(0, 0, piece)
    third = rows // TILE // 3
    lax.fori_loop(0, 2 * third, assemble, 0)
    lanes(0, 0)
    lax.fori_loop(2 * third, 3 * third, assemble, 0)
    relays(0, 0)
    bound_copy.wait()

    def turn(k, q):
        slot = k % 2
        later = k > 0
        middle = k < STEPS - 1
        weight = jnp.where(slot == 0, 1.0, 2.0)

        def gather():
            if q == 1:
                lanes(slot, q)
                relays(slot, q)
            else:
                @pl.when(later)
                def _():
                    lanes(slot, q)
                    relays(slot, q)
            collect(slot, q)
            divide(slot, q)

        if q == 0:
            gather()
        else:
            pl.when(later)(gather)
        for piece in range(PIECES):
            pl.when(later)(partial_copy(1 - slot, q, piece).wait_send)
            multiply(q, piece)
            pl.when(middle)(partial_copy(slot, q, piece).start)
        if q == 0:
            await_sends(slot, q)
        else:
            pl.when(later)(functools.partial(await_sends, slot, q))

        @pl.when(middle)
        def _():
            for piece in range(PIECES):
                partial_copy(slot, q, piece).wait_recv()
                update(slot, q, piece, weight, slot == 1)
                direct(1 - slot, q, piece)

    def step(k, carry):
        turn(k, 0)
        turn(k, 1)
        return carry

    lax.fori_loop(0, STEPS, step, 0)
    slot = (STEPS - 1) % 2
    final_ref[...] = own[slot, p]

    def gram(left, right):
        whole = lax.dot_general(
            left, right, (((0,), (0,)), ((), ())), precision=highest,
            preferred_element_type=jnp.float32,
        )
        return whole[:64] + sign_row(1.0, -1.0) * pltpu.roll(whole[64:], 64, 1)

    sums[5, 0] = gram(own[slot, 1 - p], part[1 - p])
    cross = pltpu.make_async_remote_copy(
        src_ref=sums.at[5, 0], dst_ref=arrived.at[4, 0], send_sem=g_send.at[4],
        recv_sem=g_recv.at[4], device_id=to_x, device_id_type=MESH,
    )
    cross.start()
    sums[0, 0] = gram(own[slot, p], own[slot, p])
    own_projected = gram(own[slot, p], part[p])
    cross.wait()
    sums[0, 1] = own_projected + arrived[4, 0]
    for stage, target in enumerate((to_c, to_y, to_a, to_b)):
        copy = pltpu.make_async_remote_copy(
            src_ref=sums.at[stage], dst_ref=arrived.at[stage], send_sem=g_send.at[stage],
            recv_sem=g_recv.at[stage], device_id=target, device_id_type=MESH,
        )
        copy.start()
        copy.wait()
        sums[stage + 1] = sums[stage] + arrived[stage]
    gram_ref[...] = sums[4]


def filtered(offsets, qpoints, lower_bound, upper_bound, force_constants, start_vectors):
    cells, rows, cols = force_constants.shape
    points = qpoints.shape[0]
    vmem = pl.BlockSpec(memory_space=pltpu.VMEM)
    smem = pl.BlockSpec(memory_space=pltpu.SMEM)
    dma = pltpu.SemaphoreType.DMA
    single = jnp.float32
    matrix = pltpu.VMEM((points, PIECES, 2, rows // PIECES, cols), jnp.bfloat16)
    return pl.pallas_call(
        filter_kernel,
        out_shape=(
            jax.ShapeDtypeStruct((rows, 128), single),
            jax.ShapeDtypeStruct((2, 64, 128), single),
        ),
        in_specs=[smem] * 4 + [pl.BlockSpec(memory_space=pl.ANY), vmem],
        out_specs=(vmem, vmem),
        scratch_shapes=[
            pltpu.VMEM((2, cells, TILE, cols), single),
            matrix,
            matrix,
            pltpu.VMEM((2, points, cols, 128), single),
            pltpu.VMEM((2, points, rows, 128), single),
            pltpu.VMEM((points, rows, 128), single),
            pltpu.VMEM((2, points, rows, 128), single),
            pltpu.VMEM((cols, 256), jnp.bfloat16),
            pltpu.VMEM((8, 128), single),
            pltpu.VMEM((8, 128), single),
            pltpu.VMEM((6, 2, 64, 128), single),
            pltpu.VMEM((5, 2, 64, 128), single),
            dma((2,)),
            dma((points, KINDS, PIECES)),
            dma((2, points, 8, PIECES)),
            dma((points, PIECES)),
            dma((2, points, PIECES)),
            dma((2,)),
            dma((5,)),
            dma((5,)),
        ],
        compiler_params=pltpu.CompilerParams(
            collective_id=0, has_side_effects=True, vmem_limit_bytes=56 * 1024 * 1024
        ),
    )(offsets.T, qpoints, lower_bound, upper_bound, force_constants, start_vectors)


def finish_kernel(scale, final_ref, gram_ref, basis_ref, ritz_ref):
    size = gram_ref.shape[1]
    tile = 8
    gram = [gram_ref[0, t * tile:(t + 1) * tile, :] for t in range(size // tile)]
    lane = lax.broadcasted_iota(jnp.int32, (tile, 128), 1)
    line = lax.broadcasted_iota(jnp.int32, (tile, 128), 0)
    inverse = [jnp.where(lane == line + t * tile, 1.0, 0.0) for t in range(size // tile)]
    turn = sign_row(-1.0, 1.0)
    for j in range(size):
        home, at = j // tile, j % tile
        row = gram[home][at:at + 1, :]
        pivot = row[:, j:j + 1]
        row = row / pivot
        mate = inverse[home][at:at + 1, :] / pivot
        row_turned = turn * pltpu.roll(row, 64, 1)
        mate_turned = turn * pltpu.roll(mate, 64, 1)
        for t in range(home, size // tile):
            real = gram[t][:, j:j + 1]
            imag = gram[t][:, 64 + j:65 + j]
            if t == home:
                below = line[:, :1] > at
                real = jnp.where(below, real, 0.0)
                imag = jnp.where(below, imag, 0.0)
            gram[t] = gram[t] - (real * row + imag * row_turned)
            inverse[t] = inverse[t] - (real * mate + imag * mate_turned)
    scaled = []
    for t in range(size // tile):
        diagonal = jnp.sum(jnp.where(lane == line + t * tile, gram[t], 0.0), axis=1, keepdims=True)
        scaled.append(inverse[t] / jnp.sqrt(diagonal))
    whole = jnp.concatenate(scaled, axis=0)
    paired = jnp.concatenate([whole, turn * pltpu.roll(whole, 64, 1)], axis=0)

    def against(left):
        return lax.dot_general(
            left, paired, (((1,), (1,)), ((), ())), precision=highest,
            preferred_element_type=jnp.float32,
        )

    basis_ref[...] = scale * against(final_ref[...])
    half = against(gram_ref[1])
    ritz_ref[...] = product(whole, jnp.concatenate([half, turn * pltpu.roll(half, 64, 1)], axis=0))


def finish(final_pass, grams, modes):
    vmem = pl.BlockSpec(memory_space=pltpu.VMEM)
    return pl.pallas_call(
        functools.partial(finish_kernel, math.sqrt(modes)),
        out_shape=(
            jax.ShapeDtypeStruct(final_pass.shape, jnp.float32),
            jax.ShapeDtypeStruct(grams.shape[1:], jnp.float32),
        ),
        in_specs=[vmem] * 2,
        out_specs=(vmem, vmem),
    )(final_pass, grams)


def on_block(force_constants, offsets, qpoints, lower_bound, upper_bound, start_vectors):
    final_pass, grams = filtered(
        offsets, qpoints, lower_bound, upper_bound, force_constants, start_vectors
    )
    basis_local, ritz_local = finish(final_pass, grams, MODES)
    return (basis_local[None], ritz_local[None])


def solution(mesh):
    paired = mesh.shape["pb"] == 2 and mesh.shape["row"] == 16
    return jax.shard_map(
        on_block if paired else on_device,
        mesh=mesh,
        in_specs=(P(None, "row", "pb"), P(), P(), P("pb"), P("pb"), P("row", None)),
        out_specs=(P("pb", "row", None), P("pb", None, None)),
        check_vma=False,
    )
```

```python
import functools
import math

import jax
import jax.numpy as jnp
from jax import lax
from jax.experimental import pallas as pl
from jax.experimental.pallas import tpu as pltpu
from jax.sharding import PartitionSpec as P

MODES = 4608
QDEN = 8


highest = lax.Precision.HIGHEST


def product(left, right):
    return jnp.dot(left, right, precision=highest, preferred_element_type=jnp.float32)


def inner_product(left, right):
    return lax.dot_general(
        left, right, (((0,), (0,)), ((), ())), precision=highest, preferred_element_type=jnp.float32
    )


def complex_times(left_real, left_imag, right_real, right_imag):
    return (
        product(left_real, right_real) - product(left_imag, right_imag),
        product(left_real, right_imag) + product(left_imag, right_real),
    )


def phase_table(qpoints, offsets):
    turns = jnp.sum(qpoints[:, None, :] * offsets[None, :, :], axis=2)
    turns = jnp.mod(turns, QDEN)
    angle = 2.0 * math.pi / QDEN * turns.astype(jnp.float32)
    return jnp.stack([jnp.cos(angle), jnp.sin(angle)], axis=1)


def factor_inverse(gram_real, gram_imag):
    order_size = gram_real.shape[0]
    embedded = jnp.stack(
        [jnp.stack([gram_real, -gram_imag], axis=2), jnp.stack([gram_imag, gram_real], axis=2)],
        axis=1,
    ).reshape(2 * order_size, 2 * order_size)
    lower_factor = jnp.linalg.cholesky(embedded)
    identity = jnp.eye(2 * order_size, dtype=gram_real.dtype)
    inverse = jax.scipy.linalg.solve_triangular(lower_factor, identity, lower=True)
    blocks = inverse.reshape(order_size, 2, order_size, 2)
    return (blocks[:, 0, :, 0], blocks[:, 1, :, 0])


def right_block(inverse_real, inverse_imag):
    upper_half = jnp.concatenate([inverse_real.T, -inverse_imag.T], axis=1)
    lower_half = jnp.concatenate([inverse_imag.T, inverse_real.T], axis=1)
    return jnp.concatenate([upper_half, lower_half], axis=0)


def split_gram(matrix, vector_count):
    return (
        matrix[:vector_count, :vector_count] + matrix[vector_count:, vector_count:],
        matrix[:vector_count, vector_count:] - matrix[vector_count:, :vector_count],
    )


def combine_parts(part_real, part_imag, vector_count):
    return jnp.concatenate(
        [
            part_real[:, :vector_count] - part_imag[:, vector_count:],
            part_real[:, vector_count:] + part_imag[:, :vector_count],
        ],
        axis=1,
    )


def chebyshev(vectors, apply_matrix, lower_value, upper_value, first_image):
    centre = 0.5 * (upper_value + lower_value)
    spread = 0.5 * (upper_value - lower_value)
    previous = vectors
    first_image = apply_matrix(vectors)
    current = (first_image - centre * vectors) / spread
    following = 2.0 * (apply_matrix(current) - centre * current) / spread - previous
    previous, current = (current, following)
    return current


def on_device(force_constants, offsets, qpoints, lower_bound, upper_bound, start_vectors):
    cell_count, row_count, col_count = force_constants.shape
    qcount = qpoints.shape[0]
    vector_count = start_vectors.shape[1] // 2
    coefficients = phase_table(qpoints, offsets).reshape(2 * qcount, cell_count)
    partial_value = product(
        coefficients, force_constants.reshape(cell_count, row_count * col_count)
    )
    partial_value = partial_value.reshape(qcount, 2, row_count, col_count)
    owned_block = lax.all_to_all(partial_value, "pb", split_axis=0, concat_axis=3, tiled=True)
    dyn_real = owned_block[0, 0]
    dyn_imag = owned_block[0, 1]

    def accumulate(piece):
        return combine_parts(product(dyn_real, piece), product(dyn_imag, piece), vector_count)

    def apply_matrix(vectors):
        return accumulate(lax.all_gather(vectors, "row", axis=0, tiled=True))

    lower_value = lower_bound[0]
    upper_value = upper_bound[0]
    first_pass = chebyshev(start_vectors, apply_matrix, lower_value, upper_value, None)
    final_pass = chebyshev(first_pass, apply_matrix, lower_value, upper_value, None)
    image = apply_matrix(final_pass)
    over_total, proj_total = lax.psum(
        (inner_product(final_pass, final_pass), inner_product(final_pass, image)), "row"
    )
    over_real, over_imag = split_gram(over_total, vector_count)
    proj_real, proj_imag = split_gram(proj_total, vector_count)
    inverse_real, inverse_imag = factor_inverse(over_real, over_imag)
    basis_local = math.sqrt(MODES) * product(final_pass, right_block(inverse_real, inverse_imag))
    temp_real, temp_imag = complex_times(proj_real, proj_imag, inverse_real.T, -inverse_imag.T)
    ritz_real, ritz_imag = complex_times(inverse_real, inverse_imag, temp_real, temp_imag)
    ritz_local = jnp.concatenate([ritz_real, ritz_imag], axis=1)
    return (basis_local[None], ritz_local[None])


STEPS = 5
PIECES = 2
SUBS = 3
AHEAD = ((0,), (1,), (2,))
TILE = 48
FAR, NEAR, ACROSS_Y, ACROSS_C = 0, 1, 2, 3
KINDS = 4
MESH = pl.DeviceIdType.MESH


def sign_row(first, second):
    lane = lax.broadcasted_iota(jnp.int32, (1, 128), 1)
    return jnp.where(lane < 64, first, second).astype(jnp.float32)


def eighth_cosine(turn):
    turn = turn & (QDEN - 1)
    half = math.sqrt(0.5)
    value = jnp.float32(0.0)
    for index, exact in enumerate((1.0, half, 0.0, -half, -1.0, -half, 0.0, half)):
        value = jnp.where(turn == index, jnp.float32(exact), value)
    return value


def filter_kernel(
    offsets_ref, qpoints_ref, lower_ref, upper_ref, force_ref, start_ref, final_ref, gram_ref,
    tiles, high, low, full, own, part, other, split, bounds, partner_bounds, sums, arrived,
    tile_sem, send_sem, level_recv, lane_recv, core_recv, x_send, x_recv, b_sem, g_send, g_recv,
):
    p = lax.axis_index("pb")
    row = lax.axis_index("row")
    rows = start_ref.shape[0]
    cells = force_ref.shape[0]
    cols = force_ref.shape[2]
    pairs = (cells - 1) // 2
    points = 2
    depth = rows // PIECES
    z, y, c = row // 4, (row // 2) % 2, row % 2
    group = z // 2
    owner = group == p
    not_owner = group != p
    level = z % 2
    far_piece = group + p - 2 * group * p
    to_x = (1 - p, row)
    to_c = (p, row + 1 - 2 * c)
    to_y = (p, row + 2 - 4 * y)
    to_a = (p, row + 4 - 8 * level)
    to_b = (p, (3 - z) * 4 + y * 2 + c)
    opposite = 2 - 2 * group
    to_far = [(group, (opposite + n) * 4 + y * 2 + c) for n in (0, 1)]

    def guarded(condition, action):
        if condition is None:
            action()
        else:
            pl.when(condition)(action)

    def tile_copy(index, slot):
        where = pl.ds(pl.multiple_of(index * TILE, 8), TILE)
        return pltpu.make_async_copy(
            force_ref.at[:, where, :], tiles.at[slot], tile_sem.at[slot]
        )

    tile_copy(0, 0).start()
    tile_copy(1, 1).start()

    own[0, 0] = start_ref[...]
    own[0, 1] = start_ref[...]
    own[1] = jnp.zeros((points, rows, 128), jnp.float32)
    centre = 0.5 * (upper_ref[0] + lower_ref[0])
    spread = 0.5 * (upper_ref[0] - lower_ref[0])
    line = lax.broadcasted_iota(jnp.int32, (8, 128), 0)
    bounds[...] = jnp.where(line < 4, centre, spread)

    def piece_rows(piece):
        return pl.ds(pl.multiple_of(piece * depth, 8), depth)

    grain = depth // SUBS

    def sub_rows(piece, sub):
        return pl.ds(pl.multiple_of(piece * depth + sub * grain, 8), grain)

    @pl.when(owner)
    def _():
        full[0, 0, level, y, c] = start_ref[...]

    barrier = pltpu.get_barrier_semaphore()
    around = [to_x, to_c, to_y, to_a]
    around += [(q, (opposite + n) * 4 + y * 2 + c) for q in (0, 1) for n in (0, 1)]
    for target in around:
        pl.semaphore_signal(barrier, inc=1, device_id=target, device_id_type=MESH)
    pl.semaphore_wait(barrier, len(around))

    bound_copy = pltpu.make_async_remote_copy(
        src_ref=bounds, dst_ref=partner_bounds, send_sem=b_sem.at[0], recv_sem=b_sem.at[1],
        device_id=to_x, device_id_type=MESH,
    )

    def send(source, view, q, kind, arrival, target):
        return pltpu.make_async_remote_copy(
            src_ref=source, dst_ref=view, send_sem=send_sem.at[q, kind], recv_sem=arrival,
            device_id=target, device_id_type=MESH,
        )

    def level_copy(slot, q, at_level, piece, sub, kind, target):
        where = sub_rows(piece, sub)
        return send(
            own.at[slot, q, where], full.at[slot, q, at_level, y, c, where], q, kind,
            level_recv.at[slot, q, at_level, piece, sub], target,
        )

    def lane_copy(slot, q, yy, piece, sub):
        view = full.at[slot, q, :, yy, c, sub_rows(piece, sub)]
        return send(view, view, q, ACROSS_Y, lane_recv.at[slot, q, piece, sub], to_y)

    def core_copy(slot, q, view):
        return send(view, view, q, ACROSS_C, core_recv.at[slot, q], to_c)

    def direct(slot, q, piece):
        @pl.when(far_piece == piece)
        def _():
            for sub in range(SUBS):
                for target in to_far:
                    level_copy(slot, q, level, piece, sub, FAR, target).start()

    def near(slot, q):
        @pl.when(owner)
        def _():
            for sub in range(SUBS):
                for piece in range(PIECES):
                    level_copy(slot, q, level, piece, sub, NEAR, to_a).start()

    def lanes(slot, q, sub):
        for piece in range(PIECES):
            @pl.when(not_owner)
            def _():
                level_copy(slot, q, level, piece, sub, NEAR, to_a).wait_recv()

            level_copy(slot, q, 1 - level, piece, sub, NEAR, to_a).wait_recv()
            lane_copy(slot, q, y, piece, sub).start()
        if sub == SUBS - 1:
            core_copy(slot, q, full.at[slot, q, :, y, c]).start()

    def relays(slot, q):
        for sub in range(SUBS):
            for piece in range(PIECES):
                lane_copy(slot, q, 1 - y, piece, sub).wait_recv()
                core_copy(slot, q, full.at[slot, q, :, 1 - y, c, sub_rows(piece, sub)]).start()

    def collect(slot, q):
        core_copy(slot, q, full.at[slot, q, :, :, 1 - c]).wait_recv()

    def await_sends(slot, q):
        block = own.at[slot, q]
        send(block, block, q, FAR, core_recv.at[slot, q], to_c).wait_send()

        @pl.when(owner)
        def _():
            send(block, block, q, NEAR, core_recv.at[slot, q], to_c).wait_send()

        lane = full.at[slot, q, :, y, c]
        send(lane, lane, q, ACROSS_Y, core_recv.at[slot, q], to_c).wait_send()
        half = full.at[slot, q, :, :, c]
        core_copy(slot, q, half).wait_send()

    def partial_copy(slot, q, piece):
        where = pl.ds(pl.multiple_of(piece * depth, 8), depth)
        return pltpu.make_async_remote_copy(
            src_ref=part.at[q, where], dst_ref=other.at[slot, q, where],
            send_sem=x_send.at[q, piece], recv_sem=x_recv.at[slot, q, piece],
            device_id=to_x, device_id_type=MESH,
        )

    def divide(slot, q):
        values = full[slot, q].reshape(cols, 128)
        upper = values.astype(jnp.bfloat16)
        split[:, :128] = upper
        split[:, 128:] = (values - upper.astype(jnp.float32)).astype(jnp.bfloat16)

    def multiply(q, piece):
        def stacked(ref):
            return ref[q, piece].reshape(2 * depth, cols)

        wide = jnp.dot(stacked(high), split[...], preferred_element_type=jnp.float32)
        rest = jnp.dot(stacked(low), split[:, :128], preferred_element_type=jnp.float32)
        image = wide[:, :128] + (wide[:, 128:] + rest)
        part[q, pl.ds(pl.multiple_of(piece * depth, 8), depth)] = (
            image[:depth] + sign_row(-1.0, 1.0) * pltpu.roll(image[depth:], 64, 1)
        )

    def update(slot, q, piece, weight, keep):
        mine_q = p == q
        where = pl.ds(pl.multiple_of(piece * depth, 8), depth)
        centre = jnp.where(mine_q, bounds[0:1, :], partner_bounds[0:1, :])
        spread = jnp.where(mine_q, bounds[4:5, :], partner_bounds[4:5, :])
        current = own[slot, q, where]
        previous = own[1 - slot, q, where]
        image = part[q, where] + other[slot, q, where]
        following = (image - centre * current) * (weight / spread) - jnp.where(keep, previous, 0.0)
        own[1 - slot, q, where] = following

        @pl.when(owner)
        def _():
            full[1 - slot, q, level, y, c, where] = following

    turns = [
        [
            sum(qpoints_ref[q, n] * offsets_ref[n, 1 + pair] for n in range(3))
            for pair in range(pairs)
        ]
        for q in range(points)
    ]
    cosines = [[eighth_cosine(turn) for turn in turns[q]] for q in range(points)]
    sines = [[eighth_cosine(turn - QDEN // 4) for turn in turns[q]] for q in range(points)]

    def assemble(tile, carry):
        slot = tile % 2
        tile_copy(tile, slot).wait()
        piece = tile * TILE // depth
        place = pl.ds(pl.multiple_of(tile * TILE - piece * depth, 16), TILE)
        width = 256
        for at in range(cols // width):
            span = slice(at * width, (at + 1) * width)
            real = [tiles[slot, 0, :, span]] * points
            imag = [None] * points
            for pair in range(pairs):
                first = tiles[slot, 1 + pair, :, span]
                second = tiles[slot, 1 + pair + pairs, :, span]
                total, difference = first + second, first - second
                for q in range(points):
                    real[q] = real[q] + cosines[q][pair] * total
                    term = sines[q][pair] * difference
                    imag[q] = term if pair == 0 else imag[q] + term
            for q in range(points):
                for which, value in ((0, real[q]), (1, imag[q])):
                    upper = value.astype(jnp.bfloat16)
                    high[q, piece, which, place, span] = upper
                    rest = (value - upper.astype(jnp.float32)).astype(jnp.bfloat16)
                    low[q, piece, which, place, span] = rest

        @pl.when(tile + 2 < rows // TILE)
        def _():
            tile_copy(tile + 2, slot).start()

        return carry

    bound_copy.start()
    for piece in range(PIECES):
        direct(0, 0, piece)
    near(0, 0)
    third = rows // TILE // 3
    lax.fori_loop(0, 2 * third, assemble, 0)
    for sub in range(SUBS):
        lanes(0, 0, sub)
    lax.fori_loop(2 * third, 3 * third, assemble, 0)
    bound_copy.wait()

    def apply_matrix(k, q):
        slot = k % 2
        later = k > 0
        middle = k < STEPS - 1
        other_slot, ready = (slot, later) if q == 0 else (1 - slot, middle)

        def ahead(stage):
            for sub in AHEAD[stage]:
                pl.when(ready)(functools.partial(lanes, other_slot, 1 - q, sub))

        def finish_gather():
            relays(slot, q)

        def finish_collect():
            collect(slot, q)
            divide(slot, q)

        guarded(None if q == 0 else later, finish_gather)
        ahead(0)
        guarded(None if q == 0 else later, finish_collect)
        for stage, piece in enumerate((1 - far_piece, far_piece)):
            pl.when(later)(partial_copy(1 - slot, q, piece).wait_send)
            multiply(q, piece)
            pl.when(middle)(partial_copy(slot, q, piece).start)
            ahead(1 + stage)
        guarded(None if q == 0 else later, functools.partial(await_sends, slot, q))

    def advance(k, q):
        slot = k % 2
        weight = jnp.where(slot == 0, 1.0, 2.0)
        for piece in (far_piece, 1 - far_piece):
            partial_copy(slot, q, piece).wait_recv()
            update(slot, q, piece, weight, slot == 1)
            direct(1 - slot, q, piece)
        near(1 - slot, q)

    def step(k, carry):
        for q in (0, 1):
            apply_matrix(k, q)
            pl.when(k < STEPS - 1)(functools.partial(advance, k, q))
        return carry

    lax.fori_loop(0, STEPS, step, 0)
    slot = (STEPS - 1) % 2
    final_ref[...] = own[slot, p]

    def gram(left, right):
        whole = lax.dot_general(
            left, right, (((0,), (0,)), ((), ())), precision=highest,
            preferred_element_type=jnp.float32,
        )
        return whole[:64] + sign_row(1.0, -1.0) * pltpu.roll(whole[64:], 64, 1)

    sums[5, 0] = gram(own[slot, 1 - p], part[1 - p])
    cross = pltpu.make_async_remote_copy(
        src_ref=sums.at[5, 0], dst_ref=arrived.at[4, 0], send_sem=g_send.at[4],
        recv_sem=g_recv.at[4], device_id=to_x, device_id_type=MESH,
    )
    cross.start()
    sums[0, 0] = gram(own[slot, p], own[slot, p])
    own_projected = gram(own[slot, p], part[p])
    cross.wait()
    sums[0, 1] = own_projected + arrived[4, 0]
    for stage, target in enumerate((to_c, to_y, to_a, to_b)):
        copy = pltpu.make_async_remote_copy(
            src_ref=sums.at[stage], dst_ref=arrived.at[stage], send_sem=g_send.at[stage],
            recv_sem=g_recv.at[stage], device_id=target, device_id_type=MESH,
        )
        copy.start()
        copy.wait()
        sums[stage + 1] = sums[stage] + arrived[stage]
    gram_ref[...] = sums[4]


def filtered(offsets, qpoints, lower_bound, upper_bound, force_constants, start_vectors):
    cells, rows, cols = force_constants.shape
    points = qpoints.shape[0]
    vmem = pl.BlockSpec(memory_space=pltpu.VMEM)
    smem = pl.BlockSpec(memory_space=pltpu.SMEM)
    dma = pltpu.SemaphoreType.DMA
    single = jnp.float32
    matrix = pltpu.VMEM((points, PIECES, 2, rows // PIECES, cols), jnp.bfloat16)
    return pl.pallas_call(
        filter_kernel,
        out_shape=(
            jax.ShapeDtypeStruct((rows, 128), single),
            jax.ShapeDtypeStruct((2, 64, 128), single),
        ),
        in_specs=[smem] * 4 + [pl.BlockSpec(memory_space=pl.ANY), vmem],
        out_specs=(vmem, vmem),
        scratch_shapes=[
            pltpu.VMEM((2, cells, TILE, cols), single),
            matrix,
            matrix,
            pltpu.VMEM((2, points, 2, 2, 2, rows, 128), single),
            pltpu.VMEM((2, points, rows, 128), single),
            pltpu.VMEM((points, rows, 128), single),
            pltpu.VMEM((2, points, rows, 128), single),
            pltpu.VMEM((cols, 256), jnp.bfloat16),
            pltpu.VMEM((8, 128), single),
            pltpu.VMEM((8, 128), single),
            pltpu.VMEM((6, 2, 64, 128), single),
            pltpu.VMEM((5, 2, 64, 128), single),
            dma((2,)),
            dma((points, KINDS)),
            dma((2, points, 2, PIECES, SUBS)),
            dma((2, points, PIECES, SUBS)),
            dma((2, points)),
            dma((points, PIECES)),
            dma((2, points, PIECES)),
            dma((2,)),
            dma((5,)),
            dma((5,)),
        ],
        compiler_params=pltpu.CompilerParams(
            collective_id=0, has_side_effects=True, vmem_limit_bytes=56 * 1024 * 1024
        ),
    )(offsets.T, qpoints, lower_bound, upper_bound, force_constants, start_vectors)


def finish_kernel(scale, final_ref, gram_ref, basis_ref, ritz_ref):
    size = gram_ref.shape[1]
    tile = 8
    gram = [gram_ref[0, t * tile:(t + 1) * tile, :] for t in range(size // tile)]
    lane = lax.broadcasted_iota(jnp.int32, (tile, 128), 1)
    line = lax.broadcasted_iota(jnp.int32, (tile, 128), 0)
    inverse = [jnp.where(lane == line + t * tile, 1.0, 0.0) for t in range(size // tile)]
    turn = sign_row(-1.0, 1.0)
    for j in range(size):
        home, at = j // tile, j % tile
        row = gram[home][at:at + 1, :]
        pivot = row[:, j:j + 1]
        row = row / pivot
        mate = inverse[home][at:at + 1, :] / pivot
        row_turned = turn * pltpu.roll(row, 64, 1)
        mate_turned = turn * pltpu.roll(mate, 64, 1)
        for t in range(home, size // tile):
            real = gram[t][:, j:j + 1]
            imag = gram[t][:, 64 + j:65 + j]
            if t == home:
                below = line[:, :1] > at
                real = jnp.where(below, real, 0.0)
                imag = jnp.where(below, imag, 0.0)
            gram[t] = gram[t] - (real * row + imag * row_turned)
            inverse[t] = inverse[t] - (real * mate + imag * mate_turned)
    scaled = []
    for t in range(size // tile):
        diagonal = jnp.sum(jnp.where(lane == line + t * tile, gram[t], 0.0), axis=1, keepdims=True)
        scaled.append(inverse[t] / jnp.sqrt(diagonal))
    whole = jnp.concatenate(scaled, axis=0)
    paired = jnp.concatenate([whole, turn * pltpu.roll(whole, 64, 1)], axis=0)

    def against(left):
        return lax.dot_general(
            left, paired, (((1,), (1,)), ((), ())), precision=highest,
            preferred_element_type=jnp.float32,
        )

    basis_ref[...] = scale * against(final_ref[...])
    half = against(gram_ref[1])
    ritz_ref[...] = product(whole, jnp.concatenate([half, turn * pltpu.roll(half, 64, 1)], axis=0))


def finish(final_pass, grams, modes):
    vmem = pl.BlockSpec(memory_space=pltpu.VMEM)
    return pl.pallas_call(
        functools.partial(finish_kernel, math.sqrt(modes)),
        out_shape=(
            jax.ShapeDtypeStruct(final_pass.shape, jnp.float32),
            jax.ShapeDtypeStruct(grams.shape[1:], jnp.float32),
        ),
        in_specs=[vmem] * 2,
        out_specs=(vmem, vmem),
    )(final_pass, grams)


def on_block(force_constants, offsets, qpoints, lower_bound, upper_bound, start_vectors):
    final_pass, grams = filtered(
        offsets, qpoints, lower_bound, upper_bound, force_constants, start_vectors
    )
    basis_local, ritz_local = finish(final_pass, grams, MODES)
    return (basis_local[None], ritz_local[None])


def solution(mesh):
    paired = mesh.shape["pb"] == 2 and mesh.shape["row"] == 16
    return jax.shard_map(
        on_block if paired else on_device,
        mesh=mesh,
        in_specs=(P(None, "row", "pb"), P(), P(), P("pb"), P("pb"), P("row", None)),
        out_specs=(P("pb", "row", None), P("pb", None, None)),
        check_vma=False,
    )
```

```python
import functools
import math

import jax
import jax.numpy as jnp
from jax import lax
from jax.experimental import pallas as pl
from jax.experimental.pallas import tpu as pltpu
from jax.sharding import PartitionSpec as P

MODES = 4608
QDEN = 8


highest = lax.Precision.HIGHEST


def product(left, right):
    return jnp.dot(left, right, precision=highest, preferred_element_type=jnp.float32)


def inner_product(left, right):
    return lax.dot_general(
        left, right, (((0,), (0,)), ((), ())), precision=highest, preferred_element_type=jnp.float32
    )


def complex_times(left_real, left_imag, right_real, right_imag):
    return (
        product(left_real, right_real) - product(left_imag, right_imag),
        product(left_real, right_imag) + product(left_imag, right_real),
    )


def phase_table(qpoints, offsets):
    turns = jnp.sum(qpoints[:, None, :] * offsets[None, :, :], axis=2)
    turns = jnp.mod(turns, QDEN)
    angle = 2.0 * math.pi / QDEN * turns.astype(jnp.float32)
    return jnp.stack([jnp.cos(angle), jnp.sin(angle)], axis=1)


def factor_inverse(gram_real, gram_imag):
    order_size = gram_real.shape[0]
    embedded = jnp.stack(
        [jnp.stack([gram_real, -gram_imag], axis=2), jnp.stack([gram_imag, gram_real], axis=2)],
        axis=1,
    ).reshape(2 * order_size, 2 * order_size)
    lower_factor = jnp.linalg.cholesky(embedded)
    identity = jnp.eye(2 * order_size, dtype=gram_real.dtype)
    inverse = jax.scipy.linalg.solve_triangular(lower_factor, identity, lower=True)
    blocks = inverse.reshape(order_size, 2, order_size, 2)
    return (blocks[:, 0, :, 0], blocks[:, 1, :, 0])


def right_block(inverse_real, inverse_imag):
    upper_half = jnp.concatenate([inverse_real.T, -inverse_imag.T], axis=1)
    lower_half = jnp.concatenate([inverse_imag.T, inverse_real.T], axis=1)
    return jnp.concatenate([upper_half, lower_half], axis=0)


def split_gram(matrix, vector_count):
    return (
        matrix[:vector_count, :vector_count] + matrix[vector_count:, vector_count:],
        matrix[:vector_count, vector_count:] - matrix[vector_count:, :vector_count],
    )


def combine_parts(part_real, part_imag, vector_count):
    return jnp.concatenate(
        [
            part_real[:, :vector_count] - part_imag[:, vector_count:],
            part_real[:, vector_count:] + part_imag[:, :vector_count],
        ],
        axis=1,
    )


def chebyshev(vectors, apply_matrix, lower_value, upper_value, first_image):
    centre = 0.5 * (upper_value + lower_value)
    spread = 0.5 * (upper_value - lower_value)
    previous = vectors
    first_image = apply_matrix(vectors)
    current = (first_image - centre * vectors) / spread
    following = 2.0 * (apply_matrix(current) - centre * current) / spread - previous
    previous, current = (current, following)
    return current


def on_device(force_constants, offsets, qpoints, lower_bound, upper_bound, start_vectors):
    cell_count, row_count, col_count = force_constants.shape
    qcount = qpoints.shape[0]
    vector_count = start_vectors.shape[1] // 2
    coefficients = phase_table(qpoints, offsets).reshape(2 * qcount, cell_count)
    partial_value = product(
        coefficients, force_constants.reshape(cell_count, row_count * col_count)
    )
    partial_value = partial_value.reshape(qcount, 2, row_count, col_count)
    owned_block = lax.all_to_all(partial_value, "pb", split_axis=0, concat_axis=3, tiled=True)
    dyn_real = owned_block[0, 0]
    dyn_imag = owned_block[0, 1]

    def accumulate(piece):
        return combine_parts(product(dyn_real, piece), product(dyn_imag, piece), vector_count)

    def apply_matrix(vectors):
        return accumulate(lax.all_gather(vectors, "row", axis=0, tiled=True))

    lower_value = lower_bound[0]
    upper_value = upper_bound[0]
    first_pass = chebyshev(start_vectors, apply_matrix, lower_value, upper_value, None)
    final_pass = chebyshev(first_pass, apply_matrix, lower_value, upper_value, None)
    image = apply_matrix(final_pass)
    over_total, proj_total = lax.psum(
        (inner_product(final_pass, final_pass), inner_product(final_pass, image)), "row"
    )
    over_real, over_imag = split_gram(over_total, vector_count)
    proj_real, proj_imag = split_gram(proj_total, vector_count)
    inverse_real, inverse_imag = factor_inverse(over_real, over_imag)
    basis_local = math.sqrt(MODES) * product(final_pass, right_block(inverse_real, inverse_imag))
    temp_real, temp_imag = complex_times(proj_real, proj_imag, inverse_real.T, -inverse_imag.T)
    ritz_real, ritz_imag = complex_times(inverse_real, inverse_imag, temp_real, temp_imag)
    ritz_local = jnp.concatenate([ritz_real, ritz_imag], axis=1)
    return (basis_local[None], ritz_local[None])


STEPS = 5
PIECES = 2
SUBS = 3
AHEAD = ((0,), (1,), (2,))
TILE = 48
GROUP = 3
FAR, NEAR, ACROSS_Y, ACROSS_C = 0, 1, 2, 3
KINDS = 4
MESH = pl.DeviceIdType.MESH


def sign_row(first, second):
    lane = lax.broadcasted_iota(jnp.int32, (1, 128), 1)
    return jnp.where(lane < 64, first, second).astype(jnp.float32)


def eighth_cosine(turn):
    turn = turn & (QDEN - 1)
    half = math.sqrt(0.5)
    value = jnp.float32(0.0)
    for index, exact in enumerate((1.0, half, 0.0, -half, -1.0, -half, 0.0, half)):
        value = jnp.where(turn == index, jnp.float32(exact), value)
    return value


def turned(values):
    return sign_row(-1.0, 1.0) * pltpu.roll(values, 64, 1)


def eliminate(factor, start, stop):
    size = factor.shape[1]
    tile = 8
    line = lax.broadcasted_iota(jnp.int32, (tile, 1), 0)
    first = start // tile
    pieces = [slice(t * tile, (t + 1) * tile) for t in range(size // tile)]
    gram = {t: factor[0, pieces[t]] for t in range(first, size // tile)}
    inverse = {t: factor[1, pieces[t]] for t in range(first, size // tile)}
    for j in range(start, stop):
        home, at = j // tile, j % tile
        row = gram[home][at:at + 1, :]
        mate = inverse[home][at:at + 1, :]
        row_turned, mate_turned = turned(row), turned(mate)
        scale = 1.0 / row[:, j:j + 1]
        for t in range(home, size // tile):
            real = gram[t][:, j:j + 1] * scale
            imag = gram[t][:, size + j:size + j + 1] * scale
            if t == home:
                real = jnp.where(line > at, real, 0.0)
                imag = jnp.where(line > at, imag, 0.0)
            gram[t] = gram[t] - (real * row + imag * row_turned)
            inverse[t] = inverse[t] - (real * mate + imag * mate_turned)
    for t in gram:
        factor[0, pieces[t]] = gram[t]
        factor[1, pieces[t]] = inverse[t]


def filter_kernel(
    scale,
    offsets_ref, qpoints_ref, lower_ref, upper_ref, force_ref, start_ref, basis_ref, ritz_ref,
    tiles, high, low, full, own, part, other, split, bounds, partner_bounds, sums, arrived, factor,
    tile_sem, send_sem, level_recv, lane_recv, core_recv, x_send, x_recv, b_sem, g_send, g_recv,
):
    p = lax.axis_index("pb")
    row = lax.axis_index("row")
    rows = start_ref.shape[0]
    cells = force_ref.shape[0]
    cols = force_ref.shape[2]
    pairs = (cells - 1) // 2
    points = 2
    depth = rows // PIECES
    z, y, c = row // 4, (row // 2) % 2, row % 2
    group = z // 2
    owner = group == p
    not_owner = group != p
    level = z % 2
    far_piece = group + p - 2 * group * p
    to_x = (1 - p, row)
    to_c = (p, row + 1 - 2 * c)
    to_y = (p, row + 2 - 4 * y)
    to_a = (p, row + 4 - 8 * level)
    to_b = (p, (3 - z) * 4 + y * 2 + c)
    opposite = 2 - 2 * group
    to_xc = (1 - p, row + 1 - 2 * c)
    to_ay = (p, row + 4 - 8 * level + 2 - 4 * y)
    to_z = (p, (opposite + level) * 4 + y * 2 + c)
    to_far = [(group, (opposite + n) * 4 + y * 2 + c) for n in (0, 1)]

    def guarded(condition, action):
        if condition is True:
            action()
        elif condition is not False:
            pl.when(condition)(action)

    def tile_copy(index, slot):
        where = pl.ds(pl.multiple_of(index * TILE, 8), TILE)
        return pltpu.make_async_copy(
            force_ref.at[:, where, :], tiles.at[slot], tile_sem.at[slot]
        )

    barrier = pltpu.get_barrier_semaphore()
    around = [to_x, to_c, to_y, to_a, to_xc, to_ay]
    around += [(q, (opposite + n) * 4 + y * 2 + c) for q in (0, 1) for n in (0, 1)]
    for target in around:
        pl.semaphore_signal(barrier, inc=1, device_id=target, device_id_type=MESH)

    tile_copy(0, 0).start()
    tile_copy(1, 1).start()

    own[0, 0] = start_ref[...]
    own[0, 1] = start_ref[...]
    own[1] = jnp.zeros((points, rows, 128), jnp.float32)
    centre = 0.5 * (upper_ref[0] + lower_ref[0])
    spread = 0.5 * (upper_ref[0] - lower_ref[0])
    line = lax.broadcasted_iota(jnp.int32, (8, 128), 0)
    bounds[...] = jnp.where(line < 4, centre, spread)

    def piece_rows(piece):
        return pl.ds(pl.multiple_of(piece * depth, 8), depth)

    grain = depth // SUBS

    def sub_rows(piece, sub):
        return pl.ds(pl.multiple_of(piece * depth + sub * grain, 8), grain)

    @pl.when(owner)
    def _():
        full[0, 0, level, y, c] = start_ref[...]

    pl.semaphore_wait(barrier, len(around))

    bound_copy = pltpu.make_async_remote_copy(
        src_ref=bounds, dst_ref=partner_bounds, send_sem=b_sem.at[0], recv_sem=b_sem.at[1],
        device_id=to_x, device_id_type=MESH,
    )

    def send(source, view, q, kind, arrival, target):
        return pltpu.make_async_remote_copy(
            src_ref=source, dst_ref=view, send_sem=send_sem.at[q, kind], recv_sem=arrival,
            device_id=target, device_id_type=MESH,
        )

    def level_copy(slot, q, at_level, piece, sub, kind, target):
        where = sub_rows(piece, sub)
        return send(
            own.at[slot, q, where], full.at[slot, q, at_level, y, c, where], q, kind,
            level_recv.at[slot, q, at_level, piece, sub], target,
        )

    def lane_copy(slot, q, yy, piece, sub):
        view = full.at[slot, q, :, yy, c, sub_rows(piece, sub)]
        return send(view, view, q, ACROSS_Y, lane_recv.at[slot, q, piece, sub], to_y)

    def core_copy(slot, q, view):
        return send(view, view, q, ACROSS_C, core_recv.at[slot, q], to_c)

    def tiles_of(piece):
        return [piece * (depth // TILE) + n for n in range(0, depth // TILE, GROUP)]

    def direct(slot, q, piece, group_at):
        count = SUBS * GROUP * TILE // depth

        @pl.when(far_piece == piece)
        def _():
            for sub in range(group_at * count, (group_at + 1) * count):
                for target in to_far:
                    level_copy(slot, q, level, piece, sub, FAR, target).start()

    def near(slot, q):
        @pl.when(owner)
        def _():
            for sub in range(SUBS):
                for piece in range(PIECES):
                    level_copy(slot, q, level, piece, sub, NEAR, to_a).start()

    def lanes(slot, q, sub):
        for piece in range(PIECES):
            @pl.when(not_owner)
            def _():
                level_copy(slot, q, level, piece, sub, NEAR, to_a).wait_recv()

            level_copy(slot, q, 1 - level, piece, sub, NEAR, to_a).wait_recv()
            lane_copy(slot, q, y, piece, sub).start()
        if sub == SUBS - 1:
            core_copy(slot, q, full.at[slot, q, :, y, c]).start()

    def relays(slot, q):
        for sub in range(SUBS):
            for piece in range(PIECES):
                lane_copy(slot, q, 1 - y, piece, sub).wait_recv()
                core_copy(slot, q, full.at[slot, q, :, 1 - y, c, sub_rows(piece, sub)]).start()

    def collect(slot, q):
        core_copy(slot, q, full.at[slot, q, :, :, 1 - c]).wait_recv()

    def await_sends(slot, q):
        block = own.at[slot, q]
        send(block, block, q, FAR, core_recv.at[slot, q], to_c).wait_send()

        @pl.when(owner)
        def _():
            send(block, block, q, NEAR, core_recv.at[slot, q], to_c).wait_send()

        lane = full.at[slot, q, :, y, c]
        send(lane, lane, q, ACROSS_Y, core_recv.at[slot, q], to_c).wait_send()
        half = full.at[slot, q, :, :, c]
        core_copy(slot, q, half).wait_send()

    def tile_rows(tile):
        return pl.ds(pl.multiple_of(tile * TILE, 8), GROUP * TILE)

    def partial_copy(slot, q, tile):
        where = tile_rows(tile)
        return pltpu.make_async_remote_copy(
            src_ref=part.at[q, where], dst_ref=other.at[slot, q, where],
            send_sem=x_send.at[q, tile], recv_sem=x_recv.at[slot, q, tile],
            device_id=to_x, device_id_type=MESH,
        )

    def divide(slot, q):
        values = full[slot, q].reshape(cols, 128)
        upper = values.astype(jnp.bfloat16)
        split[:, :128] = upper
        split[:, 128:] = (values - upper.astype(jnp.float32)).astype(jnp.bfloat16)

    def multiply(q, tile):
        def stacked(ref):
            return ref[q, pl.ds(tile, GROUP)].reshape(GROUP * 2 * TILE, cols)

        wide = jnp.dot(stacked(high), split[...], preferred_element_type=jnp.float32)
        rest = jnp.dot(stacked(low), split[:, :128], preferred_element_type=jnp.float32)
        image = (wide[:, :128] + (wide[:, 128:] + rest)).reshape(GROUP, 2, TILE, 128)
        crossed = turned(image[:, 1].reshape(GROUP * TILE, 128))
        part[q, tile_rows(tile)] = image[:, 0].reshape(GROUP * TILE, 128) + crossed

    def update(slot, q, tile, weight, keep):
        mine_q = p == q
        where = tile_rows(tile)
        centre = jnp.where(mine_q, bounds[0:1, :], partner_bounds[0:1, :])
        spread = jnp.where(mine_q, bounds[4:5, :], partner_bounds[4:5, :])
        current = own[slot, q, where]
        previous = own[1 - slot, q, where]
        image = part[q, where] + other[slot, q, where]
        following = (image - centre * current) * (weight / spread) - jnp.where(keep, previous, 0.0)
        own[1 - slot, q, where] = following

        @pl.when(owner)
        def _():
            full[1 - slot, q, level, y, c, where] = following

    turns = [
        [
            sum(qpoints_ref[q, n] * offsets_ref[n, 1 + pair] for n in range(3))
            for pair in range(pairs)
        ]
        for q in range(points)
    ]
    cosines = [[eighth_cosine(turn) for turn in turns[q]] for q in range(points)]
    sines = [[eighth_cosine(turn - QDEN // 4) for turn in turns[q]] for q in range(points)]

    def assemble(tile, carry):
        slot = tile % 2
        tile_copy(tile, slot).wait()
        width = 256
        lines = 16
        for at in range(TILE // lines * (cols // width)):
            start = at % (cols // width) * width
            span = slice(start, start + width)
            top = at // (cols // width) * lines
            real = [tiles[slot, 0, top:top + lines, span]] * points
            imag = [None] * points
            for pair in range(pairs):
                first = tiles[slot, 1 + pair, top:top + lines, span]
                second = tiles[slot, 1 + pair + pairs, top:top + lines, span]
                total, difference = first + second, first - second
                for q in range(points):
                    real[q] = real[q] + cosines[q][pair] * total
                    term = sines[q][pair] * difference
                    imag[q] = term if pair == 0 else imag[q] + term
            place = slice(top, top + lines)
            for q in range(points):
                for which, value in ((0, real[q]), (1, imag[q])):
                    upper = value.astype(jnp.bfloat16)
                    high[q, tile, which, place, span] = upper
                    rest = (value - upper.astype(jnp.float32)).astype(jnp.bfloat16)
                    low[q, tile, which, place, span] = rest

        @pl.when(tile + 2 < rows // TILE)
        def _():
            tile_copy(tile + 2, slot).start()

        return carry

    bound_copy.start()
    for piece in range(PIECES):
        for sub in range(depth // TILE // GROUP):
            direct(0, 0, piece, sub)
    near(0, 0)
    third = rows // TILE // 3
    lax.fori_loop(0, 2 * third, assemble, 0)
    for sub in range(SUBS):
        lanes(0, 0, sub)
    lax.fori_loop(2 * third, 3 * third, assemble, 0)
    bound_copy.wait()

    def apply_matrix(k, q, later, middle, extra=lambda stage: None):
        slot = k % 2
        wanted = True if q == 0 else later
        other_slot, ready = (slot, later) if q == 0 else (1 - slot, middle)

        def ahead(stage):
            for sub in AHEAD[stage]:
                guarded(ready, functools.partial(lanes, other_slot, 1 - q, sub))
            extra(stage)

        def take():
            collect(slot, q)
            divide(slot, q)

        guarded(wanted, functools.partial(relays, slot, q))
        ahead(0)
        guarded(wanted, take)
        for stage, piece in enumerate((1 - far_piece, far_piece)):
            for tile in tiles_of(piece):
                guarded(later, partial_copy(1 - slot, q, tile).wait_send)
                multiply(q, tile)
                guarded(middle, partial_copy(slot, q, tile).start)
            ahead(1 + stage)
        guarded(wanted, functools.partial(await_sends, slot, q))

    def advance(k, q):
        slot = k % 2
        weight = jnp.where(slot == 0, 1.0, 2.0)
        for piece in (far_piece, 1 - far_piece):
            for sub, tile in enumerate(tiles_of(piece)):
                partial_copy(slot, q, tile).wait_recv()
                update(slot, q, tile, weight, slot == 1)
                direct(1 - slot, q, piece, sub)
        near(1 - slot, q)

    def step(k, carry):
        for q in (0, 1):
            apply_matrix(k, q, k > 0, True)
            advance(k, q)
        return carry

    def gram(left, right):
        whole = lax.dot_general(
            left, right, (((0,), (0,)), ((), ())), precision=highest,
            preferred_element_type=jnp.float32,
        )
        return whole[:64] + sign_row(1.0, -1.0) * pltpu.roll(whole[64:], 64, 1)

    def sum_copy(kind, source, at, target):
        return pltpu.make_async_remote_copy(
            src_ref=sums.at[kind, source], dst_ref=arrived.at[kind, at],
            send_sem=g_send.at[kind, at], recv_sem=g_recv.at[kind, at],
            device_id=target, device_id_type=MESH,
        )

    def overlap_copy(stage):
        return sum_copy(0, stage, stage, (to_c, to_y, to_a, to_b)[stage])

    def add_overlap(stage):
        overlap_copy(stage).wait()
        sums[0, stage + 1] = sums[0, stage] + arrived[0, stage]
        if stage < 3:
            overlap_copy(stage + 1).start()

    def projected_copies(stage):
        plan = (
            ((0, 0, to_c), (5, 1, to_x), (5, 2, to_xc)),
            ((1, 3, to_y), (1, 4, to_a), (1, 5, to_ay)),
            ((2, 6, to_z),),
        )
        return [sum_copy(1, *entry) for entry in plan[stage]]

    def add_projected(stage):
        for copy in projected_copies(stage):
            copy.wait()
        if stage == 2:
            return sums[1, 2] + arrived[1, 6]
        at = 3 * stage
        sums[1, stage + 1] = (sums[1, stage] + arrived[1, at]) + (
            arrived[1, at + 1] + arrived[1, at + 2]
        )
        for copy in projected_copies(stage + 1):
            copy.start()

    lax.fori_loop(0, STEPS - 1, step, 0)
    last = STEPS - 1
    slot = last % 2
    sums[0, 0] = gram(own[slot, p], own[slot, p])
    overlap_copy(0).start()
    apply_matrix(
        last, 0, True, False,
        lambda stage: None if stage == 1 else add_overlap(min(stage, 1)),
    )
    apply_matrix(last, 1, True, False, lambda stage: add_overlap(2) if stage == 0 else None)
    sums[1, 5] = gram(own[slot, 1 - p], part[1 - p])
    sums[1, 0] = gram(own[slot, p], part[p])
    for copy in projected_copies(0):
        copy.start()
    add_overlap(3)

    lane = lax.broadcasted_iota(jnp.int32, (64, 128), 1)
    diagonal = lane == lax.broadcasted_iota(jnp.int32, (64, 128), 0)
    factor[0] = sums[0, 4]
    factor[1] = jnp.where(diagonal, 1.0, 0.0)

    def pivots(start, stop):
        pl.when(row >= 0)(functools.partial(eliminate, factor, start, stop))

    pivots(0, 22)
    add_projected(0)
    pivots(22, 44)
    add_projected(1)
    pivots(44, 64)
    kept = jnp.where(diagonal, factor[0], 0.0)
    whole = factor[1] / jnp.sqrt(jnp.sum(kept, axis=1, keepdims=True))
    paired = jnp.concatenate([whole, turned(whole)], axis=0)

    def against(left):
        return lax.dot_general(
            left, paired, (((1,), (1,)), ((), ())), precision=highest,
            preferred_element_type=jnp.float32,
        )

    basis_ref[...] = scale * against(own[slot, p])
    half = against(add_projected(2))
    ritz_ref[...] = product(whole, jnp.concatenate([half, turned(half)], axis=0))


def filtered(offsets, qpoints, lower_bound, upper_bound, force_constants, start_vectors):
    cells, rows, cols = force_constants.shape
    points = qpoints.shape[0]
    vmem = pl.BlockSpec(memory_space=pltpu.VMEM)
    smem = pl.BlockSpec(memory_space=pltpu.SMEM)
    dma = pltpu.SemaphoreType.DMA
    single = jnp.float32
    matrix = pltpu.VMEM((points, rows // TILE, 2, TILE, cols), jnp.bfloat16)
    return pl.pallas_call(
        functools.partial(filter_kernel, math.sqrt(MODES)),
        out_shape=(
            jax.ShapeDtypeStruct((rows, 128), single),
            jax.ShapeDtypeStruct((64, 128), single),
        ),
        in_specs=[smem] * 4 + [pl.BlockSpec(memory_space=pl.ANY), vmem],
        out_specs=(vmem, vmem),
        scratch_shapes=[
            pltpu.VMEM((2, cells, TILE, cols), single),
            matrix,
            matrix,
            pltpu.VMEM((2, points, 2, 2, 2, rows, 128), single),
            pltpu.VMEM((2, points, rows, 128), single),
            pltpu.VMEM((points, rows, 128), single),
            pltpu.VMEM((2, points, rows, 128), single),
            pltpu.VMEM((cols, 256), jnp.bfloat16),
            pltpu.VMEM((8, 128), single),
            pltpu.VMEM((8, 128), single),
            pltpu.VMEM((2, 6, 64, 128), single),
            pltpu.VMEM((2, 7, 64, 128), single),
            pltpu.VMEM((2, 64, 128), single),
            dma((2,)),
            dma((points, KINDS)),
            dma((2, points, 2, PIECES, SUBS)),
            dma((2, points, PIECES, SUBS)),
            dma((2, points)),
            dma((points, rows // TILE)),
            dma((2, points, rows // TILE)),
            dma((2,)),
            dma((2, 7)),
            dma((2, 7)),
        ],
        compiler_params=pltpu.CompilerParams(
            collective_id=0, has_side_effects=True, vmem_limit_bytes=56 * 1024 * 1024
        ),
    )(offsets.T, qpoints, lower_bound, upper_bound, force_constants, start_vectors)


def on_block(force_constants, offsets, qpoints, lower_bound, upper_bound, start_vectors):
    basis_local, ritz_local = filtered(
        offsets, qpoints, lower_bound, upper_bound, force_constants, start_vectors
    )
    return (basis_local[None], ritz_local[None])


def solution(mesh):
    paired = mesh.shape["pb"] == 2 and mesh.shape["row"] == 16
    return jax.shard_map(
        on_block if paired else on_device,
        mesh=mesh,
        in_specs=(P(None, "row", "pb"), P(), P(), P("pb"), P("pb"), P("row", None)),
        out_specs=(P("pb", "row", None), P("pb", None, None)),
        check_vma=False,
    )
```

```python
import functools
import math

import jax
import jax.numpy as jnp
from jax import lax
from jax.experimental import pallas as pl
from jax.experimental.pallas import tpu as pltpu
from jax.sharding import PartitionSpec as P

MODES = 4608
QDEN = 8


highest = lax.Precision.HIGHEST


def product(left, right):
    return jnp.dot(left, right, precision=highest, preferred_element_type=jnp.float32)


def inner_product(left, right):
    return lax.dot_general(
        left, right, (((0,), (0,)), ((), ())), precision=highest, preferred_element_type=jnp.float32
    )


def complex_times(left_real, left_imag, right_real, right_imag):
    return (
        product(left_real, right_real) - product(left_imag, right_imag),
        product(left_real, right_imag) + product(left_imag, right_real),
    )


def phase_table(qpoints, offsets):
    turns = jnp.sum(qpoints[:, None, :] * offsets[None, :, :], axis=2)
    turns = jnp.mod(turns, QDEN)
    angle = 2.0 * math.pi / QDEN * turns.astype(jnp.float32)
    return jnp.stack([jnp.cos(angle), jnp.sin(angle)], axis=1)


def factor_inverse(gram_real, gram_imag):
    order_size = gram_real.shape[0]
    embedded = jnp.stack(
        [jnp.stack([gram_real, -gram_imag], axis=2), jnp.stack([gram_imag, gram_real], axis=2)],
        axis=1,
    ).reshape(2 * order_size, 2 * order_size)
    lower_factor = jnp.linalg.cholesky(embedded)
    identity = jnp.eye(2 * order_size, dtype=gram_real.dtype)
    inverse = jax.scipy.linalg.solve_triangular(lower_factor, identity, lower=True)
    blocks = inverse.reshape(order_size, 2, order_size, 2)
    return (blocks[:, 0, :, 0], blocks[:, 1, :, 0])


def right_block(inverse_real, inverse_imag):
    upper_half = jnp.concatenate([inverse_real.T, -inverse_imag.T], axis=1)
    lower_half = jnp.concatenate([inverse_imag.T, inverse_real.T], axis=1)
    return jnp.concatenate([upper_half, lower_half], axis=0)


def split_gram(matrix, vector_count):
    return (
        matrix[:vector_count, :vector_count] + matrix[vector_count:, vector_count:],
        matrix[:vector_count, vector_count:] - matrix[vector_count:, :vector_count],
    )


def combine_parts(part_real, part_imag, vector_count):
    return jnp.concatenate(
        [
            part_real[:, :vector_count] - part_imag[:, vector_count:],
            part_real[:, vector_count:] + part_imag[:, :vector_count],
        ],
        axis=1,
    )


def chebyshev(vectors, apply_matrix, lower_value, upper_value, first_image):
    centre = 0.5 * (upper_value + lower_value)
    spread = 0.5 * (upper_value - lower_value)
    previous = vectors
    first_image = apply_matrix(vectors)
    current = (first_image - centre * vectors) / spread
    following = 2.0 * (apply_matrix(current) - centre * current) / spread - previous
    previous, current = (current, following)
    return current


def on_device(force_constants, offsets, qpoints, lower_bound, upper_bound, start_vectors):
    cell_count, row_count, col_count = force_constants.shape
    qcount = qpoints.shape[0]
    vector_count = start_vectors.shape[1] // 2
    coefficients = phase_table(qpoints, offsets).reshape(2 * qcount, cell_count)
    partial_value = product(
        coefficients, force_constants.reshape(cell_count, row_count * col_count)
    )
    partial_value = partial_value.reshape(qcount, 2, row_count, col_count)
    owned_block = lax.all_to_all(partial_value, "pb", split_axis=0, concat_axis=3, tiled=True)
    dyn_real = owned_block[0, 0]
    dyn_imag = owned_block[0, 1]

    def accumulate(piece):
        return combine_parts(product(dyn_real, piece), product(dyn_imag, piece), vector_count)

    def apply_matrix(vectors):
        return accumulate(lax.all_gather(vectors, "row", axis=0, tiled=True))

    lower_value = lower_bound[0]
    upper_value = upper_bound[0]
    first_pass = chebyshev(start_vectors, apply_matrix, lower_value, upper_value, None)
    final_pass = chebyshev(first_pass, apply_matrix, lower_value, upper_value, None)
    image = apply_matrix(final_pass)
    over_total, proj_total = lax.psum(
        (inner_product(final_pass, final_pass), inner_product(final_pass, image)), "row"
    )
    over_real, over_imag = split_gram(over_total, vector_count)
    proj_real, proj_imag = split_gram(proj_total, vector_count)
    inverse_real, inverse_imag = factor_inverse(over_real, over_imag)
    basis_local = math.sqrt(MODES) * product(final_pass, right_block(inverse_real, inverse_imag))
    temp_real, temp_imag = complex_times(proj_real, proj_imag, inverse_real.T, -inverse_imag.T)
    ritz_real, ritz_imag = complex_times(inverse_real, inverse_imag, temp_real, temp_imag)
    ritz_local = jnp.concatenate([ritz_real, ritz_imag], axis=1)
    return (basis_local[None], ritz_local[None])


STEPS = 5
PIECES = 2
SUBS = 3
AHEAD = ((0,), (1,), (2,))
TILE = 48
GROUP = 3
FAR, NEAR, ACROSS_Y, ACROSS_C = 0, 1, 2, 3
KINDS = 4
MESH = pl.DeviceIdType.MESH


def sign_row(first, second):
    lane = lax.broadcasted_iota(jnp.int32, (1, 128), 1)
    return jnp.where(lane < 64, first, second).astype(jnp.float32)


def eighth_cosine(turn):
    turn = turn & (QDEN - 1)
    half = math.sqrt(0.5)
    value = jnp.float32(0.0)
    for index, exact in enumerate((1.0, half, 0.0, -half, -1.0, -half, 0.0, half)):
        value = jnp.where(turn == index, jnp.float32(exact), value)
    return value


def turned(values):
    return sign_row(-1.0, 1.0) * pltpu.roll(values, 64, 1)


def eliminate(factor, start, stop):
    size = factor.shape[1]
    tile = 8
    line = lax.broadcasted_iota(jnp.int32, (tile, 1), 0)
    first = start // tile
    pieces = [slice(t * tile, (t + 1) * tile) for t in range(size // tile)]
    gram = {t: factor[0, pieces[t]] for t in range(first, size // tile)}
    inverse = {t: factor[1, pieces[t]] for t in range(first, size // tile)}
    for j in range(start, stop):
        home, at = j // tile, j % tile
        row = gram[home][at:at + 1, :]
        mate = inverse[home][at:at + 1, :]
        row_turned, mate_turned = turned(row), turned(mate)
        scale = 1.0 / row[:, j:j + 1]
        for t in range(home, size // tile):
            real = gram[t][:, j:j + 1] * scale
            imag = gram[t][:, size + j:size + j + 1] * scale
            if t == home:
                real = jnp.where(line > at, real, 0.0)
                imag = jnp.where(line > at, imag, 0.0)
            gram[t] = gram[t] - (real * row + imag * row_turned)
            inverse[t] = inverse[t] - (real * mate + imag * mate_turned)
    for t in gram:
        factor[0, pieces[t]] = gram[t]
        factor[1, pieces[t]] = inverse[t]


def filter_kernel(
    offsets_ref, qpoints_ref, lower_ref, upper_ref, force_ref, start_ref, final_ref, small_ref,
    tiles, high, low, full, own, part, other, split, bounds, partner_bounds, sums, arrived, factor,
    tile_sem, send_sem, level_recv, lane_recv, core_recv, x_send, x_recv, b_sem, g_send, g_recv,
):
    p = lax.axis_index("pb")
    row = lax.axis_index("row")
    rows = start_ref.shape[0]
    cells = force_ref.shape[0]
    cols = force_ref.shape[2]
    pairs = (cells - 1) // 2
    points = 2
    depth = rows // PIECES
    z, y, c = row // 4, (row // 2) % 2, row % 2
    group = z // 2
    owner = group == p
    not_owner = group != p
    level = z % 2
    far_piece = group + p - 2 * group * p
    to_x = (1 - p, row)
    to_c = (p, row + 1 - 2 * c)
    to_y = (p, row + 2 - 4 * y)
    to_a = (p, row + 4 - 8 * level)
    to_b = (p, (3 - z) * 4 + y * 2 + c)
    opposite = 2 - 2 * group
    to_xc = (1 - p, row + 1 - 2 * c)
    to_ay = (p, row + 4 - 8 * level + 2 - 4 * y)
    to_z = (p, (opposite + level) * 4 + y * 2 + c)

    def tile_copy(index, slot):
        where = pl.ds(pl.multiple_of(index * TILE, 8), TILE)
        return pltpu.make_async_copy(
            force_ref.at[:, where, :], tiles.at[slot], tile_sem.at[slot]
        )

    barrier = pltpu.get_barrier_semaphore()
    around = [to_x, to_c, to_y, to_a, to_xc, to_ay]
    around += [(q, (opposite + n) * 4 + y * 2 + c) for q in (0, 1) for n in (0, 1)]
    for target in around:
        pl.semaphore_signal(barrier, inc=1, device_id=target, device_id_type=MESH)

    tile_copy(0, 0).start()
    tile_copy(1, 1).start()

    own[0, 0] = start_ref[...]
    own[0, 1] = start_ref[...]
    own[1] = jnp.zeros((points, rows, 128), jnp.float32)
    centre = 0.5 * (upper_ref[0] + lower_ref[0])
    spread = 0.5 * (upper_ref[0] - lower_ref[0])
    line = lax.broadcasted_iota(jnp.int32, (8, 128), 0)
    bounds[...] = jnp.where(line < 4, centre, spread)

    def piece_rows(piece):
        return pl.ds(pl.multiple_of(piece * depth, 8), depth)

    grain = depth // SUBS

    def sub_rows(piece, sub):
        return pl.ds(pl.multiple_of(piece * depth + sub * grain, 8), grain)

    @pl.when(owner)
    def _():
        full[0, 0, level, y, c] = start_ref[...]

    pl.semaphore_wait(barrier, len(around))

    bound_copy = pltpu.make_async_remote_copy(
        src_ref=bounds, dst_ref=partner_bounds, send_sem=b_sem.at[0], recv_sem=b_sem.at[1],
        device_id=to_x, device_id_type=MESH,
    )

    def send(source, view, q, kind, arrival, target):
        return pltpu.make_async_remote_copy(
            src_ref=source, dst_ref=view, send_sem=send_sem.at[q, kind], recv_sem=arrival,
            device_id=target, device_id_type=MESH,
        )

    def level_copy(slot, q, at_level, piece, sub, kind, target):
        where = sub_rows(piece, sub)
        return send(
            own.at[slot, q, where], full.at[slot, q, at_level, y, c, where], q, kind,
            level_recv.at[slot, q, at_level, piece, sub], target,
        )

    def lane_copy(slot, q, yy, piece, sub):
        view = full.at[slot, q, :, yy, c, sub_rows(piece, sub)]
        return send(view, view, q, ACROSS_Y, lane_recv.at[slot, q, piece, sub], to_y)

    def core_copy(slot, q, view):
        return send(view, view, q, ACROSS_C, core_recv.at[slot, q], to_c)

    def tiles_of(piece):
        return [piece * (depth // TILE) + n for n in range(0, depth // TILE, GROUP)]

    def direct(slot, q, piece, group_at):
        to_far = [(group, (opposite + n) * 4 + y * 2 + c) for n in (0, 1)]
        count = SUBS * GROUP * TILE // depth

        @pl.when(far_piece == piece)
        def _():
            for sub in range(group_at * count, (group_at + 1) * count):
                for target in to_far:
                    level_copy(slot, q, level, piece, sub, FAR, target).start()

    def near(slot, q):
        @pl.when(owner)
        def _():
            for sub in range(SUBS):
                for piece in range(PIECES):
                    level_copy(slot, q, level, piece, sub, NEAR, to_a).start()

    def lanes(slot, q, sub):
        for piece in range(PIECES):
            @pl.when(not_owner)
            def _():
                level_copy(slot, q, level, piece, sub, NEAR, to_a).wait_recv()

            level_copy(slot, q, 1 - level, piece, sub, NEAR, to_a).wait_recv()
            lane_copy(slot, q, y, piece, sub).start()
        if sub == SUBS - 1:
            core_copy(slot, q, full.at[slot, q, :, y, c]).start()

    def relays(slot, q):
        for sub in range(SUBS):
            for piece in range(PIECES):
                lane_copy(slot, q, 1 - y, piece, sub).wait_recv()
                core_copy(slot, q, full.at[slot, q, :, 1 - y, c, sub_rows(piece, sub)]).start()

    def collect(slot, q):
        core_copy(slot, q, full.at[slot, q, :, :, 1 - c]).wait_recv()

    def await_sends(slot, q):
        block = own.at[slot, q]
        send(block, block, q, FAR, core_recv.at[slot, q], to_c).wait_send()

        @pl.when(owner)
        def _():
            send(block, block, q, NEAR, core_recv.at[slot, q], to_c).wait_send()

        lane = full.at[slot, q, :, y, c]
        send(lane, lane, q, ACROSS_Y, core_recv.at[slot, q], to_c).wait_send()
        core_copy(slot, q, full.at[slot, q, :, :, c]).wait_send()

    def tile_rows(tile):
        return pl.ds(pl.multiple_of(tile * TILE, 8), GROUP * TILE)

    def partial_copy(slot, q, tile):
        where = tile_rows(tile)
        return pltpu.make_async_remote_copy(
            src_ref=part.at[q, where], dst_ref=other.at[slot, q, where],
            send_sem=x_send.at[q, tile], recv_sem=x_recv.at[slot, q, tile],
            device_id=to_x, device_id_type=MESH,
        )

    def divide(slot, q, core):
        for at_level in (0, 1):
            for yy in (0, 1):
                values = full[slot, q, at_level, yy, core]
                upper = values.astype(jnp.bfloat16)
                index = at_level * 4 + yy * 2 + core
                where = pl.ds(pl.multiple_of(index * rows, 16), rows)
                split[where, :128] = upper
                split[where, 128:] = (values - upper.astype(jnp.float32)).astype(jnp.bfloat16)

    def multiply(q, tile):
        def stacked(ref):
            return ref[q, pl.ds(tile, GROUP)].reshape(GROUP * 2 * TILE, cols)

        wide = jnp.dot(stacked(high), split[...], preferred_element_type=jnp.float32)
        rest = jnp.dot(stacked(low), split[:, :128], preferred_element_type=jnp.float32)
        image = (wide[:, :128] + (wide[:, 128:] + rest)).reshape(GROUP, 2, TILE, 128)
        crossed = turned(image[:, 1].reshape(GROUP * TILE, 128))
        part[q, tile_rows(tile)] = image[:, 0].reshape(GROUP * TILE, 128) + crossed

    def update(slot, q, tile, weight, keep):
        mine_q = p == q
        where = tile_rows(tile)
        centre = jnp.where(mine_q, bounds[0:1, :], partner_bounds[0:1, :])
        spread = jnp.where(mine_q, bounds[4:5, :], partner_bounds[4:5, :])
        current = own[slot, q, where]
        previous = own[1 - slot, q, where]
        image = part[q, where] + other[slot, q, where]
        following = (image - centre * current) * (weight / spread) - jnp.where(keep, previous, 0.0)
        own[1 - slot, q, where] = following

        @pl.when(owner)
        def _():
            full[1 - slot, q, level, y, c, where] = following

    turns = [
        [
            sum(qpoints_ref[q, n] * offsets_ref[n, 1 + pair] for n in range(3))
            for pair in range(pairs)
        ]
        for q in range(points)
    ]
    cosines = [[eighth_cosine(turn) for turn in turns[q]] for q in range(points)]
    sines = [[eighth_cosine(turn - QDEN // 4) for turn in turns[q]] for q in range(points)]

    def assemble(tile, carry):
        slot = tile % 2
        tile_copy(tile, slot).wait()
        width = 256
        lines = 16
        for at in range(TILE // lines * (cols // width)):
            start = at % (cols // width) * width
            span = slice(start, start + width)
            top = at // (cols // width) * lines
            real = [tiles[slot, 0, top:top + lines, span]] * points
            imag = [None] * points
            for pair in range(pairs):
                first = tiles[slot, 1 + pair, top:top + lines, span]
                second = tiles[slot, 1 + pair + pairs, top:top + lines, span]
                total, difference = first + second, first - second
                for q in range(points):
                    real[q] = real[q] + cosines[q][pair] * total
                    term = sines[q][pair] * difference
                    imag[q] = term if pair == 0 else imag[q] + term
            place = slice(top, top + lines)
            for q in range(points):
                for which, value in ((0, real[q]), (1, imag[q])):
                    upper = value.astype(jnp.bfloat16)
                    high[q, tile, which, place, span] = upper
                    rest = (value - upper.astype(jnp.float32)).astype(jnp.bfloat16)
                    low[q, tile, which, place, span] = rest

        @pl.when(tile + 2 < rows // TILE)
        def _():
            tile_copy(tile + 2, slot).start()

        return carry

    bound_copy.start()
    for piece in range(PIECES):
        for sub in range(depth // TILE // GROUP):
            direct(0, 0, piece, sub)
    near(0, 0)
    third = rows // TILE // 3
    lax.fori_loop(0, 2 * third, assemble, 0)
    for sub in range(SUBS):
        lanes(0, 0, sub)
    lax.fori_loop(2 * third, 3 * third, assemble, 0)
    bound_copy.wait()

    def apply_matrix(k, q, extra):
        slot = k % 2
        later = k > 0
        middle = k < STEPS - 1
        wanted = later | (q == 0)
        other_slot = jnp.where(q == 0, slot, 1 - slot)
        ready = jnp.where(q == 0, k > 0, k < STEPS - 1)

        def ahead(stage):
            for sub in AHEAD[stage]:
                pl.when(ready)(functools.partial(lanes, other_slot, 1 - q, sub))
            extra(stage)

        def take():
            divide(slot, q, c)
            collect(slot, q)
            divide(slot, q, 1 - c)

        pl.when(wanted)(functools.partial(relays, slot, q))
        ahead(0)
        pl.when(wanted)(take)
        for stage, piece in enumerate((1 - far_piece, far_piece)):
            for tile in tiles_of(piece):
                pl.when(later)(partial_copy(1 - slot, q, tile).wait_send)
                multiply(q, tile)
                pl.when(middle)(partial_copy(slot, q, tile).start)
            ahead(1 + stage)
        pl.when(wanted)(functools.partial(await_sends, slot, q))

    def advance(k, q):
        slot = k % 2
        weight = jnp.where(slot == 0, 1.0, 2.0)
        for piece in (far_piece, 1 - far_piece):
            for sub, tile in enumerate(tiles_of(piece)):
                partial_copy(slot, q, tile).wait_recv()
                update(slot, q, tile, weight, slot == 1)
                direct(1 - slot, q, piece, sub)
        near(1 - slot, q)

    def gram(left, right):
        whole = lax.dot_general(
            left, right, (((0,), (0,)), ((), ())), precision=highest,
            preferred_element_type=jnp.float32,
        )
        return whole[:64] + sign_row(1.0, -1.0) * pltpu.roll(whole[64:], 64, 1)

    def sum_copy(kind, source, at, target):
        return pltpu.make_async_remote_copy(
            src_ref=sums.at[kind, source], dst_ref=arrived.at[kind, at],
            send_sem=g_send.at[kind, at], recv_sem=g_recv.at[kind, at],
            device_id=target, device_id_type=MESH,
        )

    def overlap_copy(stage):
        return sum_copy(0, stage, stage, (to_c, to_y, to_a, to_b)[stage])

    def add_overlap(stage):
        overlap_copy(stage).wait()
        sums[0, stage + 1] = sums[0, stage] + arrived[0, stage]
        if stage < 3:
            overlap_copy(stage + 1).start()

    def projected_copies(stage):
        plan = (
            ((0, 0, to_c), (5, 1, to_x), (5, 2, to_xc)),
            ((1, 3, to_y), (1, 4, to_a), (1, 5, to_ay)),
            ((2, 6, to_z),),
        )
        return [sum_copy(1, *entry) for entry in plan[stage]]

    def add_projected(stage):
        for copy in projected_copies(stage):
            copy.wait()
        if stage == 2:
            return sums[1, 2] + arrived[1, 6]
        at = 3 * stage
        sums[1, stage + 1] = (sums[1, stage] + arrived[1, at]) + (
            arrived[1, at + 1] + arrived[1, at + 2]
        )
        for copy in projected_copies(stage + 1):
            copy.start()

    slot = (STEPS - 1) % 2
    first_final = 2 * (STEPS - 1)

    def turn(index, carry):
        k, q = index // 2, index % 2

        @pl.when(index == first_final)
        def _():
            sums[0, 0] = gram(own[slot, p], own[slot, p])
            overlap_copy(0).start()

        def extra(stage):
            for at_turn, at_stage, number in ((0, 0, 0), (0, 2, 1), (1, 0, 2)):
                if stage == at_stage:
                    pl.when(index == first_final + at_turn)(
                        functools.partial(add_overlap, number)
                    )

        apply_matrix(k, q, extra)

        @pl.when(k == STEPS - 1)
        def _():
            at = jnp.where(p == q, 0, 5)
            sums[1, at] = gram(own[slot, q], part[q])

        @pl.when(k < STEPS - 1)
        def _():
            advance(k, q)

        return carry

    lax.fori_loop(0, 2 * STEPS, turn, 0)
    for copy in projected_copies(0):
        copy.start()
    add_overlap(3)

    lane = lax.broadcasted_iota(jnp.int32, (64, 128), 1)
    diagonal = lane == lax.broadcasted_iota(jnp.int32, (64, 128), 0)
    factor[0] = sums[0, 4]
    factor[1] = jnp.where(diagonal, 1.0, 0.0)

    def pivots(start, stop):
        pl.when(row >= 0)(functools.partial(eliminate, factor, start, stop))

    pivots(0, 22)
    add_projected(0)
    pivots(22, 44)
    add_projected(1)
    pivots(44, 64)
    kept = jnp.where(diagonal, factor[0], 0.0)
    inverse = factor[1] / jnp.sqrt(jnp.sum(kept, axis=1, keepdims=True))
    small_ref[0] = inverse
    final_ref[...] = own[slot, p]
    small_ref[1] = add_projected(2)


def filtered(offsets, qpoints, lower_bound, upper_bound, force_constants, start_vectors):
    cells, rows, cols = force_constants.shape
    points = qpoints.shape[0]
    vmem = pl.BlockSpec(memory_space=pltpu.VMEM)
    smem = pl.BlockSpec(memory_space=pltpu.SMEM)
    dma = pltpu.SemaphoreType.DMA
    single = jnp.float32
    matrix = pltpu.VMEM((points, rows // TILE, 2, TILE, cols), jnp.bfloat16)
    return pl.pallas_call(
        filter_kernel,
        out_shape=(
            jax.ShapeDtypeStruct((rows, 128), single),
            jax.ShapeDtypeStruct((2, 64, 128), single),
        ),
        in_specs=[smem] * 4 + [pl.BlockSpec(memory_space=pl.ANY), vmem],
        out_specs=(vmem, vmem),
        scratch_shapes=[
            pltpu.VMEM((2, cells, TILE, cols), single),
            matrix,
            matrix,
            pltpu.VMEM((2, points, 2, 2, 2, rows, 128), single),
            pltpu.VMEM((2, points, rows, 128), single),
            pltpu.VMEM((points, rows, 128), single),
            pltpu.VMEM((2, points, rows, 128), single),
            pltpu.VMEM((cols, 256), jnp.bfloat16),
            pltpu.VMEM((8, 128), single),
            pltpu.VMEM((8, 128), single),
            pltpu.VMEM((2, 6, 64, 128), single),
            pltpu.VMEM((2, 7, 64, 128), single),
            pltpu.VMEM((2, 64, 128), single),
            dma((2,)),
            dma((points, KINDS)),
            dma((2, points, 2, PIECES, SUBS)),
            dma((2, points, PIECES, SUBS)),
            dma((2, points)),
            dma((points, rows // TILE)),
            dma((2, points, rows // TILE)),
            dma((2,)),
            dma((2, 7)),
            dma((2, 7)),
        ],
        compiler_params=pltpu.CompilerParams(
            collective_id=0, has_side_effects=True, vmem_limit_bytes=56 * 1024 * 1024
        ),
    )(offsets.T, qpoints, lower_bound, upper_bound, force_constants, start_vectors)


def finish_kernel(scale, final_ref, small_ref, basis_ref, ritz_ref):
    inverse = small_ref[0]
    paired = jnp.concatenate([inverse, turned(inverse)], axis=0)

    def against(left):
        return lax.dot_general(
            left, paired, (((1,), (1,)), ((), ())), precision=highest,
            preferred_element_type=jnp.float32,
        )

    basis_ref[...] = scale * against(final_ref[...])
    half = against(small_ref[1])
    ritz_ref[...] = product(inverse, jnp.concatenate([half, turned(half)], axis=0))


def finish(final_pass, small):
    vmem = pl.BlockSpec(memory_space=pltpu.VMEM)
    return pl.pallas_call(
        functools.partial(finish_kernel, math.sqrt(MODES)),
        out_shape=(
            jax.ShapeDtypeStruct(final_pass.shape, jnp.float32),
            jax.ShapeDtypeStruct(small.shape[1:], jnp.float32),
        ),
        in_specs=[vmem] * 2,
        out_specs=(vmem, vmem),
    )(final_pass, small)


def on_block(force_constants, offsets, qpoints, lower_bound, upper_bound, start_vectors):
    final_pass, small = filtered(
        offsets, qpoints, lower_bound, upper_bound, force_constants, start_vectors
    )
    basis_local, ritz_local = finish(final_pass, small)
    return (basis_local[None], ritz_local[None])


def solution(mesh):
    paired = mesh.shape["pb"] == 2 and mesh.shape["row"] == 16
    return jax.shard_map(
        on_block if paired else on_device,
        mesh=mesh,
        in_specs=(P(None, "row", "pb"), P(), P(), P("pb"), P("pb"), P("row", None)),
        out_specs=(P("pb", "row", None), P("pb", None, None)),
        check_vma=False,
    )
```

```python
import functools
import math

import jax
import jax.numpy as jnp
from jax import lax
from jax.experimental import pallas as pl
from jax.experimental.pallas import tpu as pltpu
from jax.sharding import PartitionSpec as P

MODES = 4608
QDEN = 8


highest = lax.Precision.HIGHEST


def product(left, right):
    return jnp.dot(left, right, precision=highest, preferred_element_type=jnp.float32)


def inner_product(left, right):
    return lax.dot_general(
        left, right, (((0,), (0,)), ((), ())), precision=highest, preferred_element_type=jnp.float32
    )


def complex_times(left_real, left_imag, right_real, right_imag):
    return (
        product(left_real, right_real) - product(left_imag, right_imag),
        product(left_real, right_imag) + product(left_imag, right_real),
    )


def phase_table(qpoints, offsets):
    turns = jnp.sum(qpoints[:, None, :] * offsets[None, :, :], axis=2)
    turns = jnp.mod(turns, QDEN)
    angle = 2.0 * math.pi / QDEN * turns.astype(jnp.float32)
    return jnp.stack([jnp.cos(angle), jnp.sin(angle)], axis=1)


def factor_inverse(gram_real, gram_imag):
    order_size = gram_real.shape[0]
    embedded = jnp.stack(
        [jnp.stack([gram_real, -gram_imag], axis=2), jnp.stack([gram_imag, gram_real], axis=2)],
        axis=1,
    ).reshape(2 * order_size, 2 * order_size)
    lower_factor = jnp.linalg.cholesky(embedded)
    identity = jnp.eye(2 * order_size, dtype=gram_real.dtype)
    inverse = jax.scipy.linalg.solve_triangular(lower_factor, identity, lower=True)
    blocks = inverse.reshape(order_size, 2, order_size, 2)
    return (blocks[:, 0, :, 0], blocks[:, 1, :, 0])


def right_block(inverse_real, inverse_imag):
    upper_half = jnp.concatenate([inverse_real.T, -inverse_imag.T], axis=1)
    lower_half = jnp.concatenate([inverse_imag.T, inverse_real.T], axis=1)
    return jnp.concatenate([upper_half, lower_half], axis=0)


def split_gram(matrix, vector_count):
    return (
        matrix[:vector_count, :vector_count] + matrix[vector_count:, vector_count:],
        matrix[:vector_count, vector_count:] - matrix[vector_count:, :vector_count],
    )


def combine_parts(part_real, part_imag, vector_count):
    return jnp.concatenate(
        [
            part_real[:, :vector_count] - part_imag[:, vector_count:],
            part_real[:, vector_count:] + part_imag[:, :vector_count],
        ],
        axis=1,
    )


def chebyshev(vectors, apply_matrix, lower_value, upper_value, first_image):
    centre = 0.5 * (upper_value + lower_value)
    spread = 0.5 * (upper_value - lower_value)
    previous = vectors
    first_image = apply_matrix(vectors)
    current = (first_image - centre * vectors) / spread
    following = 2.0 * (apply_matrix(current) - centre * current) / spread - previous
    previous, current = (current, following)
    return current


def on_device(force_constants, offsets, qpoints, lower_bound, upper_bound, start_vectors):
    cell_count, row_count, col_count = force_constants.shape
    qcount = qpoints.shape[0]
    vector_count = start_vectors.shape[1] // 2
    coefficients = phase_table(qpoints, offsets).reshape(2 * qcount, cell_count)
    partial_value = product(
        coefficients, force_constants.reshape(cell_count, row_count * col_count)
    )
    partial_value = partial_value.reshape(qcount, 2, row_count, col_count)
    owned_block = lax.all_to_all(partial_value, "pb", split_axis=0, concat_axis=3, tiled=True)
    dyn_real = owned_block[0, 0]
    dyn_imag = owned_block[0, 1]

    def accumulate(piece):
        return combine_parts(product(dyn_real, piece), product(dyn_imag, piece), vector_count)

    def apply_matrix(vectors):
        return accumulate(lax.all_gather(vectors, "row", axis=0, tiled=True))

    lower_value = lower_bound[0]
    upper_value = upper_bound[0]
    first_pass = chebyshev(start_vectors, apply_matrix, lower_value, upper_value, None)
    final_pass = chebyshev(first_pass, apply_matrix, lower_value, upper_value, None)
    image = apply_matrix(final_pass)
    over_total, proj_total = lax.psum(
        (inner_product(final_pass, final_pass), inner_product(final_pass, image)), "row"
    )
    over_real, over_imag = split_gram(over_total, vector_count)
    proj_real, proj_imag = split_gram(proj_total, vector_count)
    inverse_real, inverse_imag = factor_inverse(over_real, over_imag)
    basis_local = math.sqrt(MODES) * product(final_pass, right_block(inverse_real, inverse_imag))
    temp_real, temp_imag = complex_times(proj_real, proj_imag, inverse_real.T, -inverse_imag.T)
    ritz_real, ritz_imag = complex_times(inverse_real, inverse_imag, temp_real, temp_imag)
    ritz_local = jnp.concatenate([ritz_real, ritz_imag], axis=1)
    return (basis_local[None], ritz_local[None])


STEPS = 5
PIECES = 2
SUBS = 6
AHEAD = ((0, 1), (2, 3), (4, 5))
TILE = 48
GROUP = 3
FAR, NEAR, ACROSS_Y, ACROSS_C = 0, 1, 2, 3
KINDS = 4
MESH = pl.DeviceIdType.MESH


def sign_row(first, second):
    lane = lax.broadcasted_iota(jnp.int32, (1, 128), 1)
    return jnp.where(lane < 64, first, second).astype(jnp.float32)


def eighth_cosine(turn):
    turn = turn & (QDEN - 1)
    half = math.sqrt(0.5)
    value = jnp.float32(0.0)
    for index, exact in enumerate((1.0, half, 0.0, -half, -1.0, -half, 0.0, half)):
        value = jnp.where(turn == index, jnp.float32(exact), value)
    return value


def turned(values):
    return sign_row(-1.0, 1.0) * pltpu.roll(values, 64, 1)


def eliminate(factor, start, stop):
    size = factor.shape[1]
    tile = 8
    line = lax.broadcasted_iota(jnp.int32, (tile, 1), 0)
    first = start // tile
    pieces = [slice(t * tile, (t + 1) * tile) for t in range(size // tile)]
    gram = {t: factor[0, pieces[t]] for t in range(first, size // tile)}
    inverse = {t: factor[1, pieces[t]] for t in range(first, size // tile)}
    for j in range(start, stop):
        home, at = j // tile, j % tile
        row = gram[home][at:at + 1, :]
        mate = inverse[home][at:at + 1, :]
        row_turned, mate_turned = turned(row), turned(mate)
        scale = 1.0 / row[:, j:j + 1]
        for t in range(home, size // tile):
            real = gram[t][:, j:j + 1] * scale
            imag = gram[t][:, size + j:size + j + 1] * scale
            if t == home:
                real = jnp.where(line > at, real, 0.0)
                imag = jnp.where(line > at, imag, 0.0)
            gram[t] = gram[t] - (real * row + imag * row_turned)
            inverse[t] = inverse[t] - (real * mate + imag * mate_turned)
    for t in gram:
        factor[0, pieces[t]] = gram[t]
        factor[1, pieces[t]] = inverse[t]


def filter_kernel(
    offsets_ref, qpoints_ref, lower_ref, upper_ref, force_ref, start_ref, final_ref, small_ref,
    tiles, high, low, full, own, part, other, split, bounds, partner_bounds, sums, arrived, factor,
    tile_sem, send_sem, level_recv, lane_recv, core_recv, x_send, x_recv, b_sem, g_send, g_recv,
):
    p = lax.axis_index("pb")
    row = lax.axis_index("row")
    rows = start_ref.shape[0]
    cells = force_ref.shape[0]
    cols = force_ref.shape[2]
    pairs = (cells - 1) // 2
    points = 2
    depth = rows // PIECES
    z, y, c = row // 4, (row // 2) % 2, row % 2
    group = z // 2
    owner = group == p
    not_owner = group != p
    level = z % 2
    far_piece = group + p - 2 * group * p
    to_x = (1 - p, row)
    to_c = (p, row + 1 - 2 * c)
    to_y = (p, row + 2 - 4 * y)
    to_a = (p, row + 4 - 8 * level)
    to_b = (p, (3 - z) * 4 + y * 2 + c)
    opposite = 2 - 2 * group
    to_xc = (1 - p, row + 1 - 2 * c)
    to_ay = (p, row + 4 - 8 * level + 2 - 4 * y)
    to_z = (p, (opposite + level) * 4 + y * 2 + c)

    def tile_copy(index, slot):
        where = pl.ds(pl.multiple_of(index * TILE, 8), TILE)
        return pltpu.make_async_copy(
            force_ref.at[:, where, :], tiles.at[slot], tile_sem.at[slot]
        )

    barrier = pltpu.get_barrier_semaphore()
    around = [to_x, to_c, to_y, to_a, to_xc, to_ay]
    around += [(q, (opposite + n) * 4 + y * 2 + c) for q in (0, 1) for n in (0, 1)]
    for target in around:
        pl.semaphore_signal(barrier, inc=1, device_id=target, device_id_type=MESH)

    tile_copy(0, 0).start()
    tile_copy(1, 1).start()

    own[0, 0] = start_ref[...]
    own[0, 1] = start_ref[...]
    own[1] = jnp.zeros((points, rows, 128), jnp.float32)
    centre = 0.5 * (upper_ref[0] + lower_ref[0])
    spread = 0.5 * (upper_ref[0] - lower_ref[0])
    line = lax.broadcasted_iota(jnp.int32, (8, 128), 0)
    bounds[...] = jnp.where(line < 4, centre, spread)

    def piece_rows(piece):
        return pl.ds(pl.multiple_of(piece * depth, 8), depth)

    grain = depth // SUBS

    def sub_rows(piece, sub):
        return pl.ds(pl.multiple_of(piece * depth + sub * grain, 8), grain)

    @pl.when(owner)
    def _():
        full[0, 0, level, y, c] = start_ref[...]

    pl.semaphore_wait(barrier, len(around))

    bound_copy = pltpu.make_async_remote_copy(
        src_ref=bounds, dst_ref=partner_bounds, send_sem=b_sem.at[0], recv_sem=b_sem.at[1],
        device_id=to_x, device_id_type=MESH,
    )

    def send(source, view, q, kind, arrival, target):
        return pltpu.make_async_remote_copy(
            src_ref=source, dst_ref=view, send_sem=send_sem.at[q, kind], recv_sem=arrival,
            device_id=target, device_id_type=MESH,
        )

    def level_copy(slot, q, at_level, piece, sub, kind, target):
        where = sub_rows(piece, sub)
        return send(
            own.at[slot, q, where], full.at[slot, q, at_level, y, c, where], q, kind,
            level_recv.at[slot, q, at_level, piece, sub], target,
        )

    def lane_copy(slot, q, yy, piece, sub):
        view = full.at[slot, q, :, yy, c, sub_rows(piece, sub)]
        return send(view, view, q, ACROSS_Y, lane_recv.at[slot, q, piece, sub], to_y)

    def core_copy(slot, q, view):
        return send(view, view, q, ACROSS_C, core_recv.at[slot, q], to_c)

    def tiles_of(piece):
        return [piece * (depth // TILE) + n for n in range(0, depth // TILE, GROUP)]

    def direct(slot, q, piece, group_at):
        to_far = [(group, (opposite + n) * 4 + y * 2 + c) for n in (0, 1)]
        count = SUBS * GROUP * TILE // depth

        @pl.when(far_piece == piece)
        def _():
            for sub in range(group_at * count, (group_at + 1) * count):
                for target in to_far:
                    level_copy(slot, q, level, piece, sub, FAR, target).start()

    def near(slot, q):
        @pl.when(owner)
        def _():
            for sub in range(SUBS):
                for piece in range(PIECES):
                    level_copy(slot, q, level, piece, sub, NEAR, to_a).start()

    def lanes(slot, q, sub):
        for piece in range(PIECES):
            @pl.when(not_owner)
            def _():
                level_copy(slot, q, level, piece, sub, NEAR, to_a).wait_recv()

            level_copy(slot, q, 1 - level, piece, sub, NEAR, to_a).wait_recv()
            lane_copy(slot, q, y, piece, sub).start()
        if sub == SUBS - 1:
            core_copy(slot, q, full.at[slot, q, :, y, c]).start()

    def relays(slot, q):
        for sub in range(SUBS):
            for piece in range(PIECES):
                lane_copy(slot, q, 1 - y, piece, sub).wait_recv()
                core_copy(slot, q, full.at[slot, q, :, 1 - y, c, sub_rows(piece, sub)]).start()

    def collect(slot, q):
        core_copy(slot, q, full.at[slot, q, :, :, 1 - c]).wait_recv()

    def await_sends(slot, q):
        block = own.at[slot, q]
        send(block, block, q, FAR, core_recv.at[slot, q], to_c).wait_send()

        @pl.when(owner)
        def _():
            send(block, block, q, NEAR, core_recv.at[slot, q], to_c).wait_send()

        lane = full.at[slot, q, :, y, c]
        send(lane, lane, q, ACROSS_Y, core_recv.at[slot, q], to_c).wait_send()
        core_copy(slot, q, full.at[slot, q, :, :, c]).wait_send()

    def tile_rows(tile):
        return pl.ds(pl.multiple_of(tile * TILE, 8), GROUP * TILE)

    def partial_copy(slot, q, tile):
        where = tile_rows(tile)
        return pltpu.make_async_remote_copy(
            src_ref=part.at[q, where], dst_ref=other.at[slot, q, where],
            send_sem=x_send.at[q, tile], recv_sem=x_recv.at[slot, q, tile],
            device_id=to_x, device_id_type=MESH,
        )

    def divide(slot, q, core):
        for at_level in (0, 1):
            for yy in (0, 1):
                values = full[slot, q, at_level, yy, core]
                upper = values.astype(jnp.bfloat16)
                index = at_level * 4 + yy * 2 + core
                where = pl.ds(pl.multiple_of(index * rows, 16), rows)
                split[where, :128] = upper
                split[where, 128:] = (values - upper.astype(jnp.float32)).astype(jnp.bfloat16)

    def multiply(q, tile):
        def stacked(ref):
            return ref[q, pl.ds(tile, GROUP)].reshape(GROUP * 2 * TILE, cols)

        wide = jnp.dot(stacked(high), split[...], preferred_element_type=jnp.float32)
        rest = jnp.dot(stacked(low), split[:, :128], preferred_element_type=jnp.float32)
        image = (wide[:, :128] + (wide[:, 128:] + rest)).reshape(GROUP, 2, TILE, 128)
        crossed = turned(image[:, 1].reshape(GROUP * TILE, 128))
        part[q, tile_rows(tile)] = image[:, 0].reshape(GROUP * TILE, 128) + crossed

    def update(slot, q, tile, weight, keep):
        mine_q = p == q
        where = tile_rows(tile)
        centre = jnp.where(mine_q, bounds[0:1, :], partner_bounds[0:1, :])
        spread = jnp.where(mine_q, bounds[4:5, :], partner_bounds[4:5, :])
        current = own[slot, q, where]
        previous = own[1 - slot, q, where]
        image = part[q, where] + other[slot, q, where]
        following = (image - centre * current) * (weight / spread) - jnp.where(keep, previous, 0.0)
        own[1 - slot, q, where] = following

        @pl.when(owner)
        def _():
            full[1 - slot, q, level, y, c, where] = following

    turns = [
        [
            sum(qpoints_ref[q, n] * offsets_ref[n, 1 + pair] for n in range(3))
            for pair in range(pairs)
        ]
        for q in range(points)
    ]
    cosines = [[eighth_cosine(turn) for turn in turns[q]] for q in range(points)]
    sines = [[eighth_cosine(turn - QDEN // 4) for turn in turns[q]] for q in range(points)]

    def assemble(tile, carry):
        slot = tile % 2
        tile_copy(tile, slot).wait()
        width = 256
        lines = 16
        for at in range(TILE // lines * (cols // width)):
            start = at % (cols // width) * width
            span = slice(start, start + width)
            top = at // (cols // width) * lines
            real = [tiles[slot, 0, top:top + lines, span]] * points
            imag = [None] * points
            for pair in range(pairs):
                first = tiles[slot, 1 + pair, top:top + lines, span]
                second = tiles[slot, 1 + pair + pairs, top:top + lines, span]
                total, difference = first + second, first - second
                for q in range(points):
                    real[q] = real[q] + cosines[q][pair] * total
                    term = sines[q][pair] * difference
                    imag[q] = term if pair == 0 else imag[q] + term
            place = slice(top, top + lines)
            for q in range(points):
                for which, value in ((0, real[q]), (1, imag[q])):
                    upper = value.astype(jnp.bfloat16)
                    high[q, tile, which, place, span] = upper
                    rest = (value - upper.astype(jnp.float32)).astype(jnp.bfloat16)
                    low[q, tile, which, place, span] = rest

        @pl.when(tile + 2 < rows // TILE)
        def _():
            tile_copy(tile + 2, slot).start()

        return carry

    bound_copy.start()
    for piece in range(PIECES):
        for sub in range(depth // TILE // GROUP):
            direct(0, 0, piece, sub)
    near(0, 0)
    third = rows // TILE // 3
    lax.fori_loop(0, 2 * third, assemble, 0)
    for sub in range(SUBS):
        lanes(0, 0, sub)
    lax.fori_loop(2 * third, 3 * third, assemble, 0)
    bound_copy.wait()

    def apply_matrix(k, q, extra):
        slot = k % 2
        later = k > 0
        middle = k < STEPS - 1
        wanted = later | (q == 0)
        other_slot = jnp.where(q == 0, slot, 1 - slot)
        ready = jnp.where(q == 0, k > 0, k < STEPS - 1)

        def ahead(stage):
            for sub in AHEAD[stage]:
                pl.when(ready)(functools.partial(lanes, other_slot, 1 - q, sub))
            extra(stage)

        def take():
            divide(slot, q, c)
            collect(slot, q)
            divide(slot, q, 1 - c)

        pl.when(wanted)(functools.partial(relays, slot, q))
        ahead(0)
        pl.when(wanted)(take)
        for stage, piece in enumerate((1 - far_piece, far_piece)):
            for tile in tiles_of(piece):
                pl.when(later)(partial_copy(1 - slot, q, tile).wait_send)
                multiply(q, tile)
                pl.when(middle)(partial_copy(slot, q, tile).start)
            ahead(1 + stage)
        pl.when(wanted)(functools.partial(await_sends, slot, q))

    def advance(k, q):
        slot = k % 2
        weight = jnp.where(slot == 0, 1.0, 2.0)
        for piece in (far_piece, 1 - far_piece):
            for sub, tile in enumerate(tiles_of(piece)):
                partial_copy(slot, q, tile).wait_recv()
                update(slot, q, tile, weight, slot == 1)
                direct(1 - slot, q, piece, sub)
        near(1 - slot, q)

    def gram(left, right):
        whole = lax.dot_general(
            left, right, (((0,), (0,)), ((), ())), precision=highest,
            preferred_element_type=jnp.float32,
        )
        return whole[:64] + sign_row(1.0, -1.0) * pltpu.roll(whole[64:], 64, 1)

    def sum_copy(kind, source, at, target):
        return pltpu.make_async_remote_copy(
            src_ref=sums.at[kind, source], dst_ref=arrived.at[kind, at],
            send_sem=g_send.at[kind, at], recv_sem=g_recv.at[kind, at],
            device_id=target, device_id_type=MESH,
        )

    def overlap_copy(stage):
        return sum_copy(0, stage, stage, (to_c, to_y, to_a, to_b)[stage])

    def add_overlap(stage):
        overlap_copy(stage).wait()
        sums[0, stage + 1] = sums[0, stage] + arrived[0, stage]
        if stage < 3:
            overlap_copy(stage + 1).start()

    def projected_copies(stage):
        plan = (
            ((0, 0, to_c), (5, 1, to_x), (5, 2, to_xc)),
            ((1, 3, to_y), (1, 4, to_a), (1, 5, to_ay)),
            ((2, 6, to_z),),
        )
        return [sum_copy(1, *entry) for entry in plan[stage]]

    def add_projected(stage):
        for copy in projected_copies(stage):
            copy.wait()
        if stage == 2:
            return sums[1, 2] + arrived[1, 6]
        at = 3 * stage
        sums[1, stage + 1] = (sums[1, stage] + arrived[1, at]) + (
            arrived[1, at + 1] + arrived[1, at + 2]
        )
        for copy in projected_copies(stage + 1):
            copy.start()

    slot = (STEPS - 1) % 2
    first_final = 2 * (STEPS - 1)

    def turn(index, carry):
        k, q = index // 2, index % 2

        @pl.when(index == first_final)
        def _():
            sums[0, 0] = gram(own[slot, p], own[slot, p])
            overlap_copy(0).start()

        def extra(stage):
            for at_turn, at_stage, number in ((0, 0, 0), (0, 2, 1), (1, 0, 2)):
                if stage == at_stage:
                    pl.when(index == first_final + at_turn)(
                        functools.partial(add_overlap, number)
                    )

        apply_matrix(k, q, extra)

        @pl.when(k == STEPS - 1)
        def _():
            at = jnp.where(p == q, 0, 5)
            sums[1, at] = gram(own[slot, q], part[q])

        @pl.when(k < STEPS - 1)
        def _():
            advance(k, q)

        return carry

    lax.fori_loop(0, 2 * STEPS, turn, 0)
    for copy in projected_copies(0):
        copy.start()
    add_overlap(3)

    lane = lax.broadcasted_iota(jnp.int32, (64, 128), 1)
    diagonal = lane == lax.broadcasted_iota(jnp.int32, (64, 128), 0)
    factor[0] = sums[0, 4]
    factor[1] = jnp.where(diagonal, 1.0, 0.0)

    def pivots(start, stop):
        pl.when(row >= 0)(functools.partial(eliminate, factor, start, stop))

    pivots(0, 22)
    add_projected(0)
    pivots(22, 44)
    add_projected(1)
    pivots(44, 64)
    kept = jnp.where(diagonal, factor[0], 0.0)
    inverse = factor[1] / jnp.sqrt(jnp.sum(kept, axis=1, keepdims=True))
    small_ref[0] = inverse
    final_ref[...] = own[slot, p]
    small_ref[1] = add_projected(2)


def filtered(offsets, qpoints, lower_bound, upper_bound, force_constants, start_vectors):
    cells, rows, cols = force_constants.shape
    points = qpoints.shape[0]
    vmem = pl.BlockSpec(memory_space=pltpu.VMEM)
    smem = pl.BlockSpec(memory_space=pltpu.SMEM)
    dma = pltpu.SemaphoreType.DMA
    single = jnp.float32
    matrix = pltpu.VMEM((points, rows // TILE, 2, TILE, cols), jnp.bfloat16)
    return pl.pallas_call(
        filter_kernel,
        out_shape=(
            jax.ShapeDtypeStruct((rows, 128), single),
            jax.ShapeDtypeStruct((2, 64, 128), single),
        ),
        in_specs=[smem] * 4 + [pl.BlockSpec(memory_space=pl.ANY), vmem],
        out_specs=(vmem, vmem),
        scratch_shapes=[
            pltpu.VMEM((2, cells, TILE, cols), single),
            matrix,
            matrix,
            pltpu.VMEM((2, points, 2, 2, 2, rows, 128), single),
            pltpu.VMEM((2, points, rows, 128), single),
            pltpu.VMEM((points, rows, 128), single),
            pltpu.VMEM((2, points, rows, 128), single),
            pltpu.VMEM((cols, 256), jnp.bfloat16),
            pltpu.VMEM((8, 128), single),
            pltpu.VMEM((8, 128), single),
            pltpu.VMEM((2, 6, 64, 128), single),
            pltpu.VMEM((2, 7, 64, 128), single),
            pltpu.VMEM((2, 64, 128), single),
            dma((2,)),
            dma((points, KINDS)),
            dma((2, points, 2, PIECES, SUBS)),
            dma((2, points, PIECES, SUBS)),
            dma((2, points)),
            dma((points, rows // TILE)),
            dma((2, points, rows // TILE)),
            dma((2,)),
            dma((2, 7)),
            dma((2, 7)),
        ],
        compiler_params=pltpu.CompilerParams(
            collective_id=0, has_side_effects=True, vmem_limit_bytes=56 * 1024 * 1024
        ),
    )(offsets.T, qpoints, lower_bound, upper_bound, force_constants, start_vectors)


def finish_kernel(scale, final_ref, small_ref, basis_ref, ritz_ref):
    inverse = small_ref[0]
    paired = jnp.concatenate([inverse, turned(inverse)], axis=0)

    def against(left):
        return lax.dot_general(
            left, paired, (((1,), (1,)), ((), ())), precision=highest,
            preferred_element_type=jnp.float32,
        )

    basis_ref[...] = scale * against(final_ref[...])
    half = against(small_ref[1])
    ritz_ref[...] = product(inverse, jnp.concatenate([half, turned(half)], axis=0))


def finish(final_pass, small):
    vmem = pl.BlockSpec(memory_space=pltpu.VMEM)
    return pl.pallas_call(
        functools.partial(finish_kernel, math.sqrt(MODES)),
        out_shape=(
            jax.ShapeDtypeStruct(final_pass.shape, jnp.float32),
            jax.ShapeDtypeStruct(small.shape[1:], jnp.float32),
        ),
        in_specs=[vmem] * 2,
        out_specs=(vmem, vmem),
    )(final_pass, small)


def on_block(force_constants, offsets, qpoints, lower_bound, upper_bound, start_vectors):
    final_pass, small = filtered(
        offsets, qpoints, lower_bound, upper_bound, force_constants, start_vectors
    )
    basis_local, ritz_local = finish(final_pass, small)
    return (basis_local[None], ritz_local[None])


def solution(mesh):
    paired = mesh.shape["pb"] == 2 and mesh.shape["row"] == 16
    return jax.shard_map(
        on_block if paired else on_device,
        mesh=mesh,
        in_specs=(P(None, "row", "pb"), P(), P(), P("pb"), P("pb"), P("row", None)),
        out_specs=(P("pb", "row", None), P("pb", None, None)),
        check_vma=False,
    )
```
